32 devices in a mesh: gx: 4 (over y, x), gy: 2 (over core), gz: 4 (over z).
Axes of the slice: x: 2, y: 2, z: 4, core: 2. Of those that a mesh axis runs over, the one named last changes fastest.
Arguments:
- fields: float32 [16, 48, 16, 512], P(None, 'gx', 'gy', 'gz'), may hold values from -6 to 6
- speeds: float32 [3, 16], replicated, may hold values from -1.5 to 1.5
- kinetics: float32 [16, 16], replicated, may hold values from -2 to 0.75
- block_rank: int32 [48], P('gx'), may hold values from 0 to 47, each once
- x_factor: float32 [48, 96], replicated, may hold values from -0.875 to 0.875
- y_factor: float32 [16, 64], P('gy'), may hold values from -1.5 to 1.5
- z_factor: float32 [512, 54], P('gz'), may hold values from -0.25 to 0.25
Outputs:
- fields_next: float32 [16, 48, 16, 512], P(None, 'gx', 'gy', 'gz')
- core: float32 [16, 96, 64, 54], P('gz', 'gx', 'gy')
The draws below stay inside these ranges and needn't reach their ends.
Inputs may be any that keep to these rules, and one draw needn't show every extreme that they name: block_rank is a permutation of the 48 x planes.
All inputs are finite; a program needn't handle non-finite values.
Results may differ from the reference program's by a relative error of at most 0.000098.
Values sent between devices are 32-bit elements; how exact they have to be, the bound alone decides.
No kernel may reach another device: no remote copies, remote signals or barrier semaphores. Data moves between devices by JAX's collectives and lax.ppermute only.
A program may use at most 128 MiB of HBM per device.

```python
import jax
import jax.numpy as jnp
from jax import lax

VARS = 16
RX = 96
RY = 64
RZ = 54
NX = 48
NY = 16
NZ = 512


def draw_speeds(key, part):
    key_size = jax.random.fold_in(key, 11)
    key_sign = jax.random.fold_in(key, 12)
    lowest = 1.3
    magnitude = jax.random.uniform(key_size, (3, VARS), jnp.float32, lowest, 1.5)
    flips = jax.random.uniform(key_sign, (3, VARS), jnp.float32, 0.0, 1.0)
    signs = jnp.where(flips < 0.5, -1.0, 1.0).astype(jnp.float32)
    return (magnitude * signs).astype(jnp.float32)


def draw_kinetics(key, part):
    key_rates = jax.random.fold_in(key, 21)
    spread = jnp.clip(0.25 * jax.random.normal(key_rates, (VARS, VARS), jnp.float32), -0.75, 0.75)
    damping = -1.25 * jnp.eye(VARS, dtype=jnp.float32)
    return (damping + spread).astype(jnp.float32)


def level_of(stream_key, shape, shards, smallest, top_value):
    loudness = 1.0
    for dim, shards_of in shards:
        draws = jax.random.uniform(jax.random.fold_in(jax.random.fold_in(stream_key, 6), dim), (shards_of,), jnp.float32, smallest / len(shards), top_value / len(shards))
        loudness = loudness * jnp.repeat(jnp.exp(draws), shape[dim] // shards_of).reshape((-1,) + (1,) * (len(shape) - 1 - dim))
    return loudness


def normal_values(own_key, shape, scale, bound, cuts=(), kind=jnp.bfloat16):
    entries = scale * jax.random.normal(own_key, shape, jnp.float32)
    if cuts:
        entries = entries * level_of(own_key, shape, cuts, -0.22, 0.18)
    return jnp.clip(entries, -bound, bound).astype(kind)


def setup_inputs(seed: int = 0) -> dict:
    key_of = jax.random.split(jax.random.key(seed), 8)
    return {
        "fields": normal_values(key_of[0], (VARS, NX, NY, NZ), 1.0, 6.0, ((1, 4), (2, 2), (3, 4)), jnp.float32),
        "speeds": draw_speeds(jax.random.fold_in(key_of[7], 71), 0),
        "kinetics": draw_kinetics(jax.random.fold_in(key_of[7], 71), 0),
        "block_rank": jax.random.permutation(key_of[3], NX).astype(jnp.int32),
        "x_factor": normal_values(key_of[4], (NX, RX), NX ** -0.5, 0.875, (), jnp.float32),
        "y_factor": normal_values(key_of[5], (NY, RY), NY ** -0.5, 1.5, ((0, 2),), jnp.float32),
        "z_factor": normal_values(key_of[6], (NZ, RZ), NZ ** -0.5, 0.25, ((0, 4),), jnp.float32),
    }


COEFFS = (0.8, -0.2, 4.0 / 105.0, -1.0 / 280.0)
TIME_STEP = 0.45


def tendency(padded, speeds, kinetics):
    extent = [padded.shape[1] - 8, padded.shape[2] - 8, padded.shape[3] - 8]

    def window(direction, offset):
        starts = [4, 4, 4]
        starts[direction] = starts[direction] + offset
        return padded[:, starts[0]:starts[0] + extent[0], starts[1]:starts[1] + extent[1], starts[2]:starts[2] + extent[2]]

    center = window(0, 0)
    result = jnp.einsum('vw,wxyz->vxyz', kinetics, center, precision=lax.Precision.HIGHEST)
    for direction in range(3):
        gradient = COEFFS[0] * (window(direction, 1) - window(direction, -1))
        for offset in range(2, 5):
            gradient = gradient + COEFFS[offset - 1] * (window(direction, offset) - window(direction, -offset))
        result = result - speeds[direction][:, None, None, None] * gradient
    return result


def padded_of(values):
    return jnp.pad(values, ((0, 0), (4, 4), (4, 4), (4, 4)))


def reference(fields, speeds, kinetics, block_rank, x_factor, y_factor, z_factor):
    section = fields + TIME_STEP * tendency(padded_of(fields), speeds, kinetics)
    fields_next = 0.5 * (fields + section + TIME_STEP * tendency(padded_of(section), speeds, kinetics))
    x_rows = x_factor[block_rank.astype(jnp.int32)]
    hp = lax.Precision.HIGHEST
    partial_z = jnp.einsum('vxyz,zc->vxyc', fields_next, z_factor, precision=hp)
    partial_x = jnp.einsum('vxyc,xa->vayc', partial_z, x_rows, precision=hp)
    core = jnp.einsum('vayc,yb->vabc', partial_x, y_factor, precision=hp)
    return fields_next, core
```

```python
import functools

import jax
import jax.numpy as jnp
import numpy as np
from jax import lax
from jax.experimental import pallas as pl
from jax.experimental.pallas import tpu as pltpu
from jax.sharding import PartitionSpec as P

COEFFS = (0.8, -0.2, 4.0 / 105.0, -1.0 / 280.0)
TIME_STEP = 0.45
REACH = len(COEFFS)
HALF = 64
HIGHEST = lax.Precision.HIGHEST
VMEM = pl.BlockSpec(memory_space=pltpu.VMEM)
SMEM = pl.BlockSpec(memory_space=pltpu.SMEM)


def call(kernel, out_shapes, in_specs, args, scratch=()):
    return pl.pallas_call(
        kernel,
        out_shape=tuple(jax.ShapeDtypeStruct(s, d) for s, d in out_shapes),
        in_specs=in_specs,
        out_specs=tuple(VMEM for _ in out_shapes),
        scratch_shapes=list(scratch),
        compiler_params=pltpu.CompilerParams(vmem_limit_bytes=56 * 2**20),
    )(*args)


def pack_z(v, values, rim_ref):
    lane = lax.broadcasted_iota(jnp.int32, values.shape, 2)
    width = values.shape[2]
    last = pltpu.roll(values, REACH * v + REACH, 2)
    first = pltpu.roll(values, width // 2 + REACH * v, 2)
    rim = rim_ref[...]
    rim = jnp.where(lane // REACH == v, last, rim)
    rim = jnp.where(lane // REACH == v + width // 2 // REACH, first, rim)
    rim_ref[...] = rim


def split_rims(v, values, low_ref, high_ref, rim_ref):
    low_ref[v] = values[:REACH]
    high_ref[v] = values[values.shape[0] - REACH :]
    pack_z(v, values, rim_ref)


def pack_kernel(f_ref, low_ref, high_ref, rim_ref):
    rim_ref[...] = jnp.zeros_like(rim_ref)

    def step(v, carry):
        split_rims(v, f_ref[v], low_ref, high_ref, rim_ref)
        return carry

    lax.fori_loop(0, f_ref.shape[0], step, 0)


def tendency_of(v, q_ref, xl_ref, xh_ref, yl_ref, yh_ref, rim_ref, dz_ref, kin_ref, speed_ref, edge_ref):
    nvars, nx, ny, nz = q_ref.shape
    q = q_ref[v]
    total = kin_ref[v, 0] * q_ref[0]
    for w in range(1, nvars):
        total = total + kin_ref[v, w] * q_ref[w]
    tall = jnp.concatenate([xl_ref[v], q, xh_ref[v]], axis=0)
    below = yl_ref[v] * edge_ref[0]
    above = yh_ref[v] * edge_ref[1]
    row = lax.broadcasted_iota(jnp.int32, q.shape, 1)
    for k in range(1, REACH + 1):
        sx = speed_ref[0, v] * COEFFS[k - 1]
        total = total - sx * (tall[REACH + k : REACH + k + nx] - tall[REACH - k : REACH - k + nx])
        ahead = pltpu.roll(jnp.where(row < k, above, q), ny - k, 1)
        behind = pltpu.roll(jnp.where(row >= ny - k, below, q), k, 1)
        total = total - (speed_ref[1, v] * COEFFS[k - 1]) * (ahead - behind)
    rims = pltpu.roll(rim_ref[...].reshape(nx * ny, nz), lax.rem(nz - REACH * v, nz), 1)
    pair = jnp.concatenate([q.reshape(nx * ny, nz), rims], axis=1)
    gz = jnp.dot(pair, dz_ref[...], precision=HIGHEST, preferred_element_type=jnp.float32)
    return total - speed_ref[2, v] * gz.reshape(nx, ny, nz)


def join_rims(zl_ref, zh_ref, rim_ref):
    lane = lax.broadcasted_iota(jnp.int32, rim_ref.shape, 2)
    rim_ref[...] = jnp.where(lane < rim_ref.shape[2] // 2, zl_ref[...], zh_ref[...])


def section_kernel(
    f_ref, xl_ref, xh_ref, yl_ref, yh_ref, zl_ref, zh_ref, dz_ref, kin_ref, speed_ref, edge_ref,
    s_ref, low_ref, high_ref, out_rim_ref, rim_ref,
):
    join_rims(zl_ref, zh_ref, rim_ref)
    out_rim_ref[...] = jnp.zeros_like(out_rim_ref)

    def step(v, carry):
        rate = tendency_of(v, f_ref, xl_ref, xh_ref, yl_ref, yh_ref, rim_ref, dz_ref, kin_ref, speed_ref, edge_ref)
        s = f_ref[v] + TIME_STEP * rate
        s_ref[v] = s
        split_rims(v, s, low_ref, high_ref, out_rim_ref)
        return carry

    lax.fori_loop(0, f_ref.shape[0], step, 0)


def next_kernel(
    f_ref, s_ref, xl_ref, xh_ref, yl_ref, yh_ref, zl_ref, zh_ref, dz_ref, zf_ref, kin_ref, speed_ref, edge_ref,
    next_ref, proj_ref, rim_ref,
):
    nvars, nx, ny, nz = f_ref.shape
    join_rims(zl_ref, zh_ref, rim_ref)

    def step(p, carry):
        both = []
        for v in (2 * p, 2 * p + 1):
            rate = tendency_of(v, s_ref, xl_ref, xh_ref, yl_ref, yh_ref, rim_ref, dz_ref, kin_ref, speed_ref, edge_ref)
            new = 0.5 * (f_ref[v] + s_ref[v] + TIME_STEP * rate)
            next_ref[v] = new
            both.append(new.reshape(nx * ny, nz))
        pair = jnp.concatenate(both, axis=1)
        proj_ref[p] = jnp.dot(pair, zf_ref[...], precision=HIGHEST, preferred_element_type=jnp.float32)
        return carry

    lax.fori_loop(0, nvars // 2, step, 0)


def split_bf16(x):
    high = x.astype(jnp.bfloat16)
    return high, (x - high.astype(jnp.float32)).astype(jnp.bfloat16)


def factor_kernel(rank_ref, row_ref, xf_ref, yf_ref, high_ref, low_ref, xt_ref):
    width = rank_ref.shape[1]
    pick = lax.broadcasted_iota(jnp.int32, (xf_ref.shape[1], width), 0) == rank_ref[...]
    xt_ref[...] = jnp.dot(xf_ref[...], pick.astype(jnp.float32), precision=HIGHEST, preferred_element_type=jnp.float32)
    pick = lax.broadcasted_iota(jnp.int32, (yf_ref.shape[1], width), 0) == row_ref[...]
    yt = jnp.dot(yf_ref[...], pick.astype(jnp.float32), precision=HIGHEST, preferred_element_type=jnp.float32)
    ny = yt.shape[0]
    for a in range(xt_ref.shape[0]):
        high, low = split_bf16(xt_ref[a : a + 1, :] * yt)
        high_ref[a * ny : (a + 1) * ny, :] = high
        low_ref[a * ny : (a + 1) * ny, :] = low


def core_kernel(high_ref, low_ref, *refs):
    out_ref = refs[-1]
    pairs = refs[0].shape[0]
    rank = out_ref.shape[2]
    columns = [jnp.concatenate([r[p] for r in refs[:-1]], axis=0) for p in range(pairs)]
    high, low = split_bf16(jnp.concatenate(columns, axis=1))
    dot = functools.partial(jnp.dot, preferred_element_type=jnp.float32)
    result = dot(high_ref[...], high) + (dot(high_ref[...], low) + dot(low_ref[...], high))
    for v in range(2 * pairs):
        out_ref[v] = result[:, v * HALF : v * HALF + rank]


def shifted(x, axis, count, k):
    return lax.ppermute(x, axis, [(i, (i + k) % count) for i in range(count)])


def gathered(x, axis):
    count = lax.axis_size(axis)
    if count <= 4:
        return [x] + [shifted(x, axis, count, k) for k in range(1, count)]
    blocks = lax.all_gather(x, axis)
    return [blocks[k] for k in range(count)]


def both_ways(low, high, axis):
    ends = lax.axis_size(axis) - 1
    from_low = lax.ppermute(high, axis, [(i, i + 1) for i in range(ends)])
    from_high = lax.ppermute(low, axis, [(i + 1, i) for i in range(ends)])
    return from_low, from_high


def beside(block, axis):
    if lax.axis_size(axis) == 2:
        other = lax.ppermute(block, axis, [(0, 1), (1, 0)])
        return other, other
    return both_ways(block, block, axis)


def derivative_matrix(nz):
    matrix = np.zeros((2 * nz, nz), np.float32)
    for k in range(1, REACH + 1):
        for z in range(nz):
            for source, sign in ((z + k, 1.0), (z - k, -1.0)):
                if source >= nz:
                    source = nz + nz // 2 + source - nz
                elif source < 0:
                    source = nz + REACH + source
                matrix[source, z] += sign * COEFFS[k - 1]
    return matrix


def local(fields, speeds, kinetics, block_rank, x_factor, y_factor, z_factor):
    nvars, nx, ny, nz = fields.shape
    rank = z_factor.shape[1]
    gz = lax.axis_size("gz")
    f32, bf16 = jnp.float32, jnp.bfloat16
    rim = (nvars, REACH, ny, nz)
    plane = (nx, ny, nz)
    dz = jnp.asarray(derivative_matrix(nz))
    iy = lax.axis_index("gy")
    edges = jnp.stack([iy > 0, iy < lax.axis_size("gy") - 1]).astype(f32)

    low, high, packed = call(pack_kernel, [(rim, f32), (rim, f32), (plane, f32)], [VMEM], (fields,))
    yl, yh = beside(fields, "gy")
    xl, xh = both_ways(low, high, "gx")
    zl, zh = both_ways(packed, packed, "gz")
    section, low, high, packed = call(
        section_kernel,
        [(fields.shape, f32), (rim, f32), (rim, f32), (plane, f32)],
        [VMEM] * 8 + [SMEM] * 3,
        (fields, xl, xh, yl, yh, zl, zh, dz, kinetics, speeds, edges),
        [pltpu.VMEM(plane, f32)],
    )
    yl, yh = beside(section, "gy")
    xl, xh = both_ways(low, high, "gx")
    zl, zh = both_ways(packed, packed, "gz")
    zero = jnp.zeros((nz, HALF), f32)
    wide = jnp.pad(z_factor, ((0, 0), (0, HALF - rank)))
    zf = jnp.concatenate([jnp.concatenate([wide, zero], 1), jnp.concatenate([zero, wide], 1)], 0)
    fields_next, proj = call(
        next_kernel,
        [(fields.shape, f32), ((nvars // 2, nx * ny, 2 * HALF), f32)],
        [VMEM] * 10 + [SMEM] * 3,
        (fields, section, xl, xh, yl, yh, zl, zh, dz, zf, kinetics, speeds, edges),
        [pltpu.VMEM(plane, f32)],
    )

    ranks = jnp.stack(gathered(block_rank, "gx"))
    y_rows = jnp.concatenate(gathered(y_factor, "gy"), axis=0)
    blocks_y = lax.axis_size("gy")
    shape = (ranks.shape[0], blocks_y, nx, ny)
    rank_of = jnp.broadcast_to(ranks[:, None, :, None], shape).reshape(1, -1)
    row_ids = jnp.arange(blocks_y * ny, dtype=jnp.int32).reshape(1, blocks_y, 1, ny)
    row_of = jnp.broadcast_to(row_ids, shape).reshape(1, -1)
    a_count = x_factor.shape[1] // lax.axis_size("gx")
    b_count = y_factor.shape[1] // blocks_y
    xf = lax.dynamic_slice_in_dim(x_factor, lax.axis_index("gx") * a_count, a_count, 1).T
    yf = lax.dynamic_slice_in_dim(y_rows, iy * b_count, b_count, 1).T
    cells = rank_of.shape[1]
    q_high, q_low = call(
        factor_kernel,
        [((a_count * b_count, cells), bf16)] * 2,
        [VMEM] * 4,
        (rank_of, row_of, xf, yf),
        [pltpu.VMEM((a_count, cells), f32)],
    )

    pairs = nvars // 2 // gz
    chunks = proj.reshape(gz, pairs, nx * ny, 2 * HALF)
    iz = lax.axis_index("gz")
    own = lax.dynamic_index_in_dim(chunks, iz, 0, keepdims=False)
    for k in range(1, gz):
        piece = lax.dynamic_index_in_dim(chunks, lax.rem(iz + k, gz), 0, keepdims=False)
        own = own + shifted(piece, "gz", gz, k)
    parts = []
    for block in gathered(own, "gx"):
        parts += gathered(block, "gy")
    (core,) = call(
        core_kernel,
        [((2 * pairs, a_count * b_count, rank), f32)],
        [VMEM] * (2 + len(parts)),
        (q_high, q_low, *parts),
    )
    return fields_next, core.reshape(2 * pairs, a_count, b_count, rank)


def solution(mesh):
    placed = (P(None, "gx", "gy", "gz"), P(), P(), P("gx"), P(), P("gy", None), P("gz", None))
    return jax.shard_map(
        local,
        mesh=mesh,
        in_specs=placed,
        out_specs=(P(None, "gx", "gy", "gz"), P("gz", "gx", "gy", None)),
        check_vma=False,
    )
```

```python
import functools

import jax
import jax.numpy as jnp
import numpy as np
from jax import lax
from jax.experimental import pallas as pl
from jax.experimental.pallas import tpu as pltpu
from jax.sharding import PartitionSpec as P

COEFFS = (0.8, -0.2, 4.0 / 105.0, -1.0 / 280.0)
SCALE = 840.0
WHOLE = (672.0, -168.0, 32.0, -3.0)
TIME_STEP = 0.45
REACH = len(COEFFS)
HALF = 64
F32, BF16 = jnp.float32, jnp.bfloat16
HIGHEST = lax.Precision.HIGHEST
VMEM = pl.BlockSpec(memory_space=pltpu.VMEM)
SMEM = pl.BlockSpec(memory_space=pltpu.SMEM)


def call(kernel, out_shapes, in_specs, args, scratch=(), room=16):
    return pl.pallas_call(
        kernel,
        out_shape=tuple(jax.ShapeDtypeStruct(s, d) for s, d in out_shapes),
        in_specs=in_specs,
        out_specs=tuple(VMEM for _ in out_shapes),
        scratch_shapes=list(scratch),
        compiler_params=pltpu.CompilerParams(vmem_limit_bytes=room * 2**20),
    )(*args)


def dot(a, b):
    return jnp.dot(a, b, preferred_element_type=F32)


def exact(a, b, dims=((1,), (0,))):
    return lax.dot_general(a, b, (dims, ((), ())), precision=HIGHEST, preferred_element_type=F32)


def split(x):
    high = x.astype(BF16)
    return high, (x - high.astype(F32)).astype(BF16)


def split_rims(v, values, low_ref, high_ref, rim_ref):
    low_ref[v] = values[:REACH]
    high_ref[v] = values[values.shape[0] - REACH :]
    width = values.shape[2]
    group = lax.shift_right_logical(lax.broadcasted_iota(jnp.int32, values.shape, 2), 2)
    last = pltpu.roll(values, REACH * v + REACH, 2)
    first = pltpu.roll(values, width // 2 + REACH * v, 2)
    rim = jnp.where(group == v, last, rim_ref[...])
    rim_ref[...] = jnp.where(group == v + width // 2 // REACH, first, rim)


def pack_kernel(f_ref, low_ref, high_ref, rim_ref):
    rim_ref[...] = jnp.zeros_like(rim_ref)

    def step(v, carry):
        split_rims(v, f_ref[v], low_ref, high_ref, rim_ref)
        return carry

    lax.fori_loop(0, f_ref.shape[0], step, 0)


def weight_kernel(kin_ref, speed_ref, edge_ref, unit_ref, shift_ref, zf_ref, w_ref, zf_out_ref, wide_ref):
    nvars = kin_ref.shape[0]
    rows, columns = unit_ref.shape
    row_v = lax.broadcasted_iota(jnp.int32, (rows, nvars), 0) // (rows // nvars)
    spread = (row_v == lax.broadcasted_iota(jnp.int32, (rows, nvars), 1)).astype(F32)
    column_v = lax.broadcasted_iota(jnp.int32, (nvars, columns), 1) // (columns // nvars)
    gather = (column_v == lax.broadcasted_iota(jnp.int32, (nvars, columns), 0)).astype(F32)
    rates = exact(exact(spread, kin_ref[...]), gather)
    speed = exact(spread, speed_ref[...], ((1,), (1,)))[:, 1:2]
    shifts = shift_ref[0] + edge_ref[0] * shift_ref[1] + edge_ref[1] * shift_ref[2]
    high, low = split(TIME_STEP * (rates * unit_ref[...] - speed * shifts))
    w_ref[0:rows] = high
    w_ref[rows:] = low
    depth = zf_ref.shape[0]
    wide_ref[...] = jnp.zeros_like(wide_ref)
    wide_ref[:, 0 : zf_ref.shape[1]] = zf_ref[...]
    high, low = split(wide_ref[...])
    zf_out_ref[0:depth, 0 : 2 * HALF] = high
    zf_out_ref[0:depth, 2 * HALF :] = low
    high, low = split(pltpu.roll(wide_ref[...], HALF, 1))
    zf_out_ref[depth:, 0 : 2 * HALF] = high
    zf_out_ref[depth:, 2 * HALF :] = low


def mix_planes(q_ref, beside_ref, w_ref, rate_ref):
    nvars, nx, ny, nz = q_ref.shape
    rows = nvars * ny

    def step(i, carry):
        high, low = [], []
        for p in (2 * i, 2 * i + 1):
            cells = jnp.concatenate([q_ref[:, p], beside_ref[:, p]], axis=1)
            h, l = split(cells.reshape(2 * rows, nz))
            high.append(h)
            low.append(l)
        both = dot(w_ref[...], jnp.concatenate(high, axis=1))
        total = both[:rows] + both[rows:] + dot(w_ref[0:rows], jnp.concatenate(low, axis=1))
        for j in range(2):
            rate_ref[:, 2 * i + j] = total[:, j * nz : (j + 1) * nz].reshape(nvars, ny, nz)
        return carry

    lax.fori_loop(0, nx // 2, step, 0)


def join_rims(zl_ref, zh_ref, shift_ref, rim_ref):
    nx, ny, nz = rim_ref.shape
    lane = lax.broadcasted_iota(jnp.int32, rim_ref.shape, 2)
    rim = jnp.where(lane < nz // 2, zl_ref[...], zh_ref[...]).reshape(nx * ny, nz)
    high, low = split(rim)
    rim_ref[...] = (dot(high, shift_ref[...]) + dot(low, shift_ref[...])).reshape(rim_ref.shape)


def step_of(v, q_ref, xl_ref, xh_ref, dz_ref, rate_ref, rim_ref, speed_ref):
    nvars, nx, ny, nz = q_ref.shape
    q = q_ref[v]
    tall = jnp.concatenate([xl_ref[v], q, xh_ref[v]], axis=0)
    gx = None
    for k in range(1, REACH + 1):
        part = COEFFS[k - 1] * (tall[REACH + k : REACH + k + nx] - tall[REACH - k : REACH - k + nx])
        gx = part if gx is None else gx + part
    high, low = split(q.reshape(nx * ny, nz))
    gz = dot(jnp.concatenate([high, low], axis=1), dz_ref[...]).reshape(nx, ny, nz)
    lane = lax.broadcasted_iota(jnp.int32, q.shape, 2)
    rim = rim_ref[...]
    first = pltpu.roll(rim, lax.rem(nz - REACH * v, nz), 2)
    last = pltpu.roll(rim, nz // 2 - REACH - REACH * v, 2)
    gz = gz + jnp.where(lane < REACH, first, jnp.where(lane >= nz - REACH, last, 0.0))
    return rate_ref[v] - (TIME_STEP * speed_ref[0, v]) * gx - (TIME_STEP / SCALE * speed_ref[2, v]) * gz


def section_kernel(
    f_ref, xl_ref, xh_ref, beside_ref, zl_ref, zh_ref, w_ref, dz_ref, shift_ref, speed_ref,
    s_ref, low_ref, high_ref, out_rim_ref, rate_ref, rim_ref,
):
    mix_planes(f_ref, beside_ref, w_ref, rate_ref)
    join_rims(zl_ref, zh_ref, shift_ref, rim_ref)
    out_rim_ref[...] = jnp.zeros_like(out_rim_ref)

    def step(v, carry):
        s = f_ref[v] + step_of(v, f_ref, xl_ref, xh_ref, dz_ref, rate_ref, rim_ref, speed_ref)
        s_ref[v] = s
        split_rims(v, s, low_ref, high_ref, out_rim_ref)
        return carry

    lax.fori_loop(0, f_ref.shape[0], step, 0)


def next_kernel(
    f_ref, s_ref, xl_ref, xh_ref, beside_ref, zl_ref, zh_ref, w_ref, dz_ref, shift_ref, zf_ref, speed_ref,
    next_ref, proj_ref, rate_ref, rim_ref,
):
    nvars, nx, ny, nz = f_ref.shape
    mix_planes(s_ref, beside_ref, w_ref, rate_ref)
    join_rims(zl_ref, zh_ref, shift_ref, rim_ref)

    def step(p, carry):
        both = []
        for v in (2 * p, 2 * p + 1):
            rate = step_of(v, s_ref, xl_ref, xh_ref, dz_ref, rate_ref, rim_ref, speed_ref)
            new = 0.5 * (f_ref[v] + s_ref[v] + rate)
            next_ref[v] = new
            both.append(new.reshape(nx * ny, nz))
        high, low = split(jnp.concatenate(both, axis=1))
        wide = dot(high, zf_ref[...])
        proj_ref[p] = wide[:, : 2 * HALF] + wide[:, 2 * HALF :] + dot(low, zf_ref[:, : 2 * HALF])
        return carry

    lax.fori_loop(0, nvars // 2, step, 0)


def factor_kernel(rank_ref, place_ref, xf_ref, *refs):
    y_refs, (out_ref, xt_ref) = refs[:-2], refs[-2:]
    planes, a_count = rank_ref.shape[1], xt_ref.shape[0]
    ny = y_refs[0].shape[0]
    width = planes * ny
    b_count = out_ref.shape[1] // a_count

    def own(count, total, place):
        column = lax.broadcasted_iota(jnp.int32, (count, total), 1)
        return (column == lax.broadcasted_iota(jnp.int32, (count, total), 0) + place * count).astype(F32)

    mine = exact(own(a_count, xf_ref.shape[1], place_ref[0]), xf_ref[...], ((1,), (1,)))
    pick = lax.broadcasted_iota(jnp.int32, (xf_ref.shape[0], planes), 0) == rank_ref[...]
    mine = exact(mine, pick.astype(F32))
    column = lax.broadcasted_iota(jnp.int32, (planes, width), 1)
    spread = lax.broadcasted_iota(jnp.int32, (planes, width), 0) == column // ny
    xt_ref[...] = exact(mine, spread.astype(F32))
    column = lax.broadcasted_iota(jnp.int32, (ny, width), 1)
    spread = lax.broadcasted_iota(jnp.int32, (ny, width), 0) == lax.rem(column, ny)
    for i, y_ref in enumerate(y_refs):
        rows = exact(own(b_count, y_ref.shape[1], place_ref[1]), y_ref[...], ((1,), (1,)))
        yt = exact(rows, spread.astype(F32))
        for a in range(a_count):
            high, low = split(xt_ref[a : a + 1, :] * yt)
            out_ref[0, a * b_count : (a + 1) * b_count, i * width : (i + 1) * width] = high
            out_ref[1, a * b_count : (a + 1) * b_count, i * width : (i + 1) * width] = low


def core_kernel(q_ref, *refs):
    out_ref = refs[-1]
    pairs = refs[0].shape[0]
    rank = out_ref.shape[2]
    columns = [jnp.concatenate([r[p] for r in refs[:-1]], axis=0) for p in range(pairs)]
    high, low = split(jnp.concatenate(columns, axis=1))
    result = dot(q_ref[0], high) + (dot(q_ref[0], low) + dot(q_ref[1], high))
    for v in range(2 * pairs):
        out_ref[v] = result[:, v * HALF : v * HALF + rank]


def shifted(x, axis, count, k):
    return lax.ppermute(x, axis, [(i, (i + k) % count) for i in range(count)])


def gathered(x, axis):
    count = lax.axis_size(axis)
    if count <= 4:
        return [x] + [shifted(x, axis, count, k) for k in range(1, count)]
    blocks = lax.all_gather(x, axis)
    return [blocks[k] for k in range(count)]


def both_ways(low, high, axis):
    ends = lax.axis_size(axis) - 1
    from_low = lax.ppermute(high, axis, [(i, i + 1) for i in range(ends)])
    from_high = lax.ppermute(low, axis, [(i + 1, i) for i in range(ends)])
    return from_low, from_high


def beside(block, axis):
    if lax.axis_size(axis) == 2:
        return lax.ppermute(block, axis, [(0, 1), (1, 0)])
    from_low, from_high = both_ways(block, block, axis)
    row = lax.broadcasted_iota(jnp.int32, block.shape, 2)
    return jnp.where(row < REACH, from_high, from_low)


def derivative_matrix(nz):
    matrix = np.zeros((nz, nz), np.float32)
    for k in range(1, REACH + 1):
        for z in range(nz):
            if z + k < nz:
                matrix[z + k, z] += WHOLE[k - 1]
            if z - k >= 0:
                matrix[z - k, z] -= WHOLE[k - 1]
    return np.concatenate([matrix, matrix], axis=0)


def rim_matrix(nvars, nz):
    matrix = np.zeros((nz, nz), np.float32)
    for v in range(nvars):
        for source in range(REACH):
            for target in range(REACH):
                left, right = target + REACH - source, source + REACH - target
                first, last = REACH * v, nz // 2 + REACH * v
                if left <= REACH:
                    matrix[first + source, first + target] -= WHOLE[left - 1]
                if right <= REACH:
                    matrix[last + source, last + target] += WHOLE[right - 1]
    return matrix


def y_matrices(nvars, ny):
    unit = np.zeros((nvars, ny, nvars, 2, ny), np.float32)
    shifts = np.zeros((3, nvars, ny, nvars, 2, ny), np.float32)
    for y in range(ny):
        unit[:, y, :, 0, y] = 1.0
        for k in range(1, REACH + 1):
            for source, sign in ((y + k, 1.0), (y - k, -1.0)):
                for v in range(nvars):
                    if source >= ny:
                        shifts[2, v, y, v, 1, source - ny] += sign * COEFFS[k - 1]
                    elif source < 0:
                        shifts[1, v, y, v, 1, source + ny] += sign * COEFFS[k - 1]
                    else:
                        shifts[0, v, y, v, 0, source] += sign * COEFFS[k - 1]
    return unit.reshape(nvars * ny, -1), shifts.reshape(3, nvars * ny, -1)


def local(fields, speeds, kinetics, block_rank, x_factor, y_factor, z_factor):
    nvars, nx, ny, nz = fields.shape
    rank = z_factor.shape[1]
    gx, gy, gz = (lax.axis_size(axis) for axis in ("gx", "gy", "gz"))
    ix, iy, iz = (lax.axis_index(axis) for axis in ("gx", "gy", "gz"))
    rim = (nvars, REACH, ny, nz)
    plane = (nx, ny, nz)
    dz = jnp.asarray(derivative_matrix(nz), BF16)
    rim_shift = jnp.asarray(rim_matrix(nvars, nz), BF16)
    unit, shifts = y_matrices(nvars, ny)
    edges = jnp.stack([iy > 0, iy < gy - 1]).astype(F32)
    places = jnp.stack([ix, iy]).astype(jnp.int32)
    scratch = [pltpu.VMEM(fields.shape, F32), pltpu.VMEM(plane, F32)]

    low, high, packed = call(pack_kernel, [(rim, F32), (rim, F32), (plane, F32)], [VMEM], (fields,))
    xl, xh = both_ways(low, high, "gx")
    zl, zh = both_ways(packed, packed, "gz")
    other = beside(fields, "gy")
    weights, zf = call(
        weight_kernel,
        [((2 * nvars * ny, 2 * nvars * ny), BF16), ((2 * nz, 4 * HALF), BF16)],
        [VMEM, VMEM, SMEM, VMEM, VMEM, VMEM],
        (kinetics, speeds, edges, unit, shifts, z_factor),
        [pltpu.VMEM((nz, 2 * HALF), F32)],
    )
    section, low, high, packed = call(
        section_kernel,
        [(fields.shape, F32), (rim, F32), (rim, F32), (plane, F32)],
        [VMEM] * 9 + [SMEM],
        (fields, xl, xh, other, zl, zh, weights, dz, rim_shift, speeds),
        scratch,
    )
    xl, xh = both_ways(low, high, "gx")
    zl, zh = both_ways(packed, packed, "gz")
    other = beside(section, "gy")
    fields_next, proj = call(
        next_kernel,
        [(fields.shape, F32), ((nvars // 2, nx * ny, 2 * HALF), F32)],
        [VMEM] * 11 + [SMEM],
        (fields, section, xl, xh, other, zl, zh, weights, dz, rim_shift, zf, speeds),
        scratch,
    )

    ranks = jnp.concatenate(gathered(block_rank.reshape(1, nx), "gx"), axis=1)
    y_rows = gathered(y_factor, "gy")
    a_count, b_count = x_factor.shape[1] // gx, y_factor.shape[1] // gy
    cells = gx * nx * gy * ny
    (factor,) = call(
        factor_kernel,
        [((2, a_count * b_count, cells), BF16)],
        [VMEM, SMEM, VMEM] + [VMEM] * gy,
        (ranks, places, x_factor, *y_rows),
        [pltpu.VMEM((a_count, gx * nx * ny), F32)],
    )

    pairs = nvars // 2 // gz
    chunks = proj.reshape(gz, pairs, nx * ny, 2 * HALF)
    own = lax.dynamic_index_in_dim(chunks, iz, 0, keepdims=False)
    for k in range(1, gz):
        piece = lax.dynamic_index_in_dim(chunks, lax.rem(iz + k, gz), 0, keepdims=False)
        own = own + shifted(piece, "gz", gz, k)
    blocks = [gathered(block, "gy") for block in gathered(own, "gx")]
    parts = [blocks[i][j] for j in range(gy) for i in range(gx)]
    (core,) = call(
        core_kernel,
        [((2 * pairs, a_count * b_count, rank), F32)],
        [VMEM] * (1 + len(parts)),
        (factor, *parts),
        room=16 if cells <= 1024 else 50,
    )
    return fields_next, core.reshape(2 * pairs, a_count, b_count, rank)


def solution(mesh):
    placed = (P(None, "gx", "gy", "gz"), P(), P(), P("gx"), P(), P("gy", None), P("gz", None))
    return jax.shard_map(
        local,
        mesh=mesh,
        in_specs=placed,
        out_specs=(P(None, "gx", "gy", "gz"), P("gz", "gx", "gy", None)),
        check_vma=False,
    )
```

```python
import functools

import jax
import jax.numpy as jnp
from jax import lax
from jax.experimental import pallas as pl
from jax.experimental.pallas import tpu as pltpu
from jax.sharding import PartitionSpec as P

COEFFS = (0.8, -0.2, 4.0 / 105.0, -1.0 / 280.0)
SCALE = 840.0
WHOLE = (672.0, -168.0, 32.0, -3.0)
TIME_STEP = 0.45
REACH = len(COEFFS)
HALF = 64
F32, BF16 = jnp.float32, jnp.bfloat16
HIGHEST = lax.Precision.HIGHEST
VMEM = pl.BlockSpec(memory_space=pltpu.VMEM)
SMEM = pl.BlockSpec(memory_space=pltpu.SMEM)


def call(kernel, out_shapes, in_specs, args, scratch=(), room=16):
    return pl.pallas_call(
        kernel,
        out_shape=tuple(jax.ShapeDtypeStruct(s, d) for s, d in out_shapes),
        in_specs=in_specs,
        out_specs=tuple(VMEM for _ in out_shapes),
        scratch_shapes=list(scratch),
        compiler_params=pltpu.CompilerParams(vmem_limit_bytes=room * 2**20),
    )(*args)


def dot(a, b):
    return jnp.dot(a, b, preferred_element_type=F32)


def exact(a, b, dims=((1,), (0,))):
    return lax.dot_general(a, b, (dims, ((), ())), precision=HIGHEST, preferred_element_type=F32)


def split(x):
    high = x.astype(BF16)
    return high, (x - high.astype(F32)).astype(BF16)


def rim_kernel(f_ref, low_ref, high_ref, sems):
    top = f_ref.shape[1] - REACH
    copies = [
        pltpu.make_async_copy(f_ref.at[:, pl.ds(start, REACH)], target, sems.at[i])
        for i, (start, target) in enumerate(((0, low_ref), (top, high_ref)))
    ]
    for copy in copies:
        copy.start()
    for copy in copies:
        copy.wait()


def pack_rim(v, values, rim_ref):
    width = values.shape[2]
    group = lax.shift_right_logical(lax.broadcasted_iota(jnp.int32, values.shape, 2), 2)
    last = pltpu.roll(values, REACH * v + REACH, 2)
    first = pltpu.roll(values, width // 2 + REACH * v, 2)
    rim = jnp.where(group == v, last, rim_ref[...])
    rim_ref[...] = jnp.where(group == v + width // 2 // REACH, first, rim)


def pack_kernel(f_ref, rim_ref):
    rim_ref[...] = jnp.zeros_like(rim_ref)

    def step(v, carry):
        pack_rim(v, f_ref[v], rim_ref)
        return carry

    lax.fori_loop(0, f_ref.shape[0], step, 0, unroll=4)


def iota(shape, dim):
    return lax.broadcasted_iota(jnp.int32, shape, dim)


def low_bits(x, size):
    return lax.rem(x, jnp.int32(size))


def weight_kernel(kin_ref, speed_ref, zf_ref, w_ref, zf_out_ref, dz_ref, shift_ref, scale_ref, wide_ref):
    nvars = kin_ref.shape[0]
    rows, columns = w_ref.shape[0] // 2, w_ref.shape[1]
    ny = rows // nvars
    spread = (iota((rows, nvars), 0) // ny == iota((rows, nvars), 1)).astype(F32)
    gather = (iota((nvars, columns), 1) // (2 * ny) == iota((nvars, columns), 0)).astype(F32)
    rates = exact(exact(spread, kin_ref[...]), gather)
    speed = exact(spread, speed_ref[...], ((1,), (1,)))[:, 1:2]
    row, column = iota((rows, columns), 0), iota((rows, columns), 1)
    y, other = low_bits(row, ny), low_bits(column, 2 * ny)
    iy = lax.axis_index("gy")
    below, above = iy > 0, iy < lax.axis_size("gy") - 1
    far = 8 * ny
    up = jnp.where(above, other - y, far)
    down = jnp.where(below, other - 2 * ny - y, far)
    offset = jnp.where(other < ny, other - y, jnp.where(other < ny + REACH, up, down))
    shifts = jnp.zeros((rows, columns), F32)
    for k in range(1, REACH + 1):
        shifts = jnp.where(offset == k, COEFFS[k - 1], jnp.where(offset == -k, -COEFFS[k - 1], shifts))
    shifts = jnp.where(row // ny == column // (2 * ny), speed * shifts, 0.0)
    high, low = split(TIME_STEP * (jnp.where(other == y, rates, 0.0) - shifts))
    w_ref[0:rows] = high
    w_ref[rows:] = low

    depth, rank = zf_ref.shape[1], zf_ref.shape[0]
    identity = (iota((depth, depth), 0) == iota((depth, depth), 1)).astype(F32)
    wide_ref[...] = jnp.zeros_like(wide_ref)
    wide_ref[:, 0:rank] = exact(identity, zf_ref[...], ((1,), (1,)))
    high, low = split(wide_ref[...])
    zf_out_ref[0:depth, 0 : 2 * HALF] = high
    zf_out_ref[0:depth, 2 * HALF :] = low
    high, low = split(pltpu.roll(wide_ref[...], HALF, 1))
    zf_out_ref[depth:, 0 : 2 * HALF] = high
    zf_out_ref[depth:, 2 * HALF :] = low

    source, target = iota((depth, depth), 0), iota((depth, depth), 1)
    offset = source - target
    inner = jnp.zeros((depth, depth), F32)
    for k in range(1, REACH + 1):
        inner = jnp.where(offset == k, WHOLE[k - 1], jnp.where(offset == -k, -WHOLE[k - 1], inner))
    dz_ref[0:depth] = inner.astype(BF16)
    dz_ref[depth:] = inner.astype(BF16)
    turn = low_bits(target, REACH) - low_bits(source, REACH)
    first = source < depth // 2
    offset = REACH + jnp.where(first, turn, -turn)
    outer = jnp.zeros((depth, depth), F32)
    for k in range(1, REACH + 1):
        outer = jnp.where(offset == k, WHOLE[k - 1], outer)
    outer = jnp.where(source // REACH == target // REACH, jnp.where(first, -outer, outer), 0.0)
    shift_ref[...] = outer.astype(BF16)

    tile = scale_ref.shape[2:]
    for v in range(nvars):
        scale_ref[v, 0] = jnp.broadcast_to(TIME_STEP * speed_ref[0:1, v : v + 1], tile)
        scale_ref[v, 1] = jnp.broadcast_to(TIME_STEP / SCALE * speed_ref[2:3, v : v + 1], tile)


def mix_planes(q_ref, beside_ref, w_ref, rate_ref):
    nvars, nx, ny, nz = q_ref.shape
    rows = nvars * ny

    def step(i, carry):
        high, low = [], []
        for p in (2 * i, 2 * i + 1):
            cells = jnp.concatenate([q_ref[:, p], beside_ref[:, p]], axis=1)
            h, l = split(cells.reshape(2 * rows, nz))
            high.append(h)
            low.append(l)
        both = dot(w_ref[...], jnp.concatenate(high, axis=1))
        total = both[:rows] + both[rows:] + dot(w_ref[0:rows], jnp.concatenate(low, axis=1))
        for j in range(2):
            rate_ref[:, 2 * i + j] = total[:, j * nz : (j + 1) * nz].reshape(nvars, ny, nz)
        return carry

    lax.fori_loop(0, nx // 2, step, 0, unroll=True)


def join_rims(zl_ref, zh_ref, shift_ref, rim_ref):
    nx, ny, nz = rim_ref.shape
    lane = lax.broadcasted_iota(jnp.int32, rim_ref.shape, 2)
    rim = jnp.where(lane < nz // 2, zl_ref[...], zh_ref[...]).reshape(nx * ny, nz)
    high, low = split(rim)
    rim_ref[...] = (dot(high, shift_ref[...]) + dot(low, shift_ref[...])).reshape(rim_ref.shape)


def step_of(v, q_ref, xl_ref, xh_ref, dz_ref, rate_ref, rim_ref, scale_ref):
    nvars, nx, ny, nz = q_ref.shape
    q = q_ref[v]
    tall = jnp.concatenate([xl_ref[v], q, xh_ref[v]], axis=0)
    gx = None
    for k in range(1, REACH + 1):
        part = COEFFS[k - 1] * (tall[REACH + k : REACH + k + nx] - tall[REACH - k : REACH - k + nx])
        gx = part if gx is None else gx + part
    high, low = split(q.reshape(nx * ny, nz))
    gz = dot(jnp.concatenate([high, low], axis=1), dz_ref[...]).reshape(nx, ny, nz)
    lane = lax.broadcasted_iota(jnp.int32, q.shape, 2)
    rim = rim_ref[...]
    first = pltpu.roll(rim, lax.rem(nz - REACH * v, nz), 2)
    last = pltpu.roll(rim, nz // 2 - REACH - REACH * v, 2)
    gz = gz + jnp.where(lane < REACH, first, jnp.where(lane >= nz - REACH, last, 0.0))
    return rate_ref[v] - scale_ref[v, 0] * gx - scale_ref[v, 1] * gz


def section_kernel(
    f_ref, xl_ref, xh_ref, beside_ref, zl_ref, zh_ref, w_ref, dz_ref, shift_ref, scale_ref,
    s_ref, low_ref, high_ref, out_rim_ref, rate_ref, rim_ref,
):
    mix_planes(f_ref, beside_ref, w_ref, rate_ref)
    join_rims(zl_ref, zh_ref, shift_ref, rim_ref)
    out_rim_ref[...] = jnp.zeros_like(out_rim_ref)

    def step(v, carry):
        s = f_ref[v] + step_of(v, f_ref, xl_ref, xh_ref, dz_ref, rate_ref, rim_ref, scale_ref)
        s_ref[v] = s
        low_ref[v] = s[:REACH]
        high_ref[v] = s[s.shape[0] - REACH :]
        pack_rim(v, s, out_rim_ref)
        return carry

    lax.fori_loop(0, f_ref.shape[0], step, 0, unroll=4)


def next_kernel(
    f_ref, s_ref, xl_ref, xh_ref, beside_ref, zl_ref, zh_ref, w_ref, dz_ref, shift_ref, zf_ref, scale_ref,
    next_ref, proj_ref, rate_ref, rim_ref,
):
    nvars, nx, ny, nz = f_ref.shape
    mix_planes(s_ref, beside_ref, w_ref, rate_ref)
    join_rims(zl_ref, zh_ref, shift_ref, rim_ref)

    def step(p, carry):
        both = []
        for v in (2 * p, 2 * p + 1):
            rate = step_of(v, s_ref, xl_ref, xh_ref, dz_ref, rate_ref, rim_ref, scale_ref)
            new = 0.5 * (f_ref[v] + s_ref[v] + rate)
            next_ref[v] = new
            both.append(new.reshape(nx * ny, nz))
        high, low = split(jnp.concatenate(both, axis=1))
        wide = dot(high, zf_ref[...])
        proj_ref[p] = wide[:, : 2 * HALF] + wide[:, 2 * HALF :] + dot(low, zf_ref[:, : 2 * HALF])
        return carry

    lax.fori_loop(0, nvars // 2, step, 0, unroll=2)


def factor_kernel(rank_ref, xf_ref, *refs):
    y_refs, (out_ref, xt_ref) = refs[:-2], refs[-2:]
    planes, a_count = rank_ref.shape[1], xt_ref.shape[0]
    ny = y_refs[0].shape[0]
    width = planes * ny
    b_count = out_ref.shape[1] // a_count

    def own(count, total, place):
        column = lax.broadcasted_iota(jnp.int32, (count, total), 1)
        return (column == lax.broadcasted_iota(jnp.int32, (count, total), 0) + place * count).astype(F32)

    mine = exact(own(a_count, xf_ref.shape[1], lax.axis_index("gx")), xf_ref[...], ((1,), (1,)))
    pick = lax.broadcasted_iota(jnp.int32, (xf_ref.shape[0], planes), 0) == rank_ref[...]
    mine = exact(mine, pick.astype(F32))
    column = lax.broadcasted_iota(jnp.int32, (planes, width), 1)
    spread = lax.broadcasted_iota(jnp.int32, (planes, width), 0) == column // ny
    xt_ref[...] = exact(mine, spread.astype(F32))
    column = lax.broadcasted_iota(jnp.int32, (ny, width), 1)
    spread = lax.broadcasted_iota(jnp.int32, (ny, width), 0) == lax.rem(column, ny)
    for i, y_ref in enumerate(y_refs):
        rows = exact(own(b_count, y_ref.shape[1], lax.axis_index("gy")), y_ref[...], ((1,), (1,)))
        yt = exact(rows, spread.astype(F32))
        for a in range(a_count):
            high, low = split(xt_ref[a : a + 1, :] * yt)
            out_ref[0, a * b_count : (a + 1) * b_count, i * width : (i + 1) * width] = high
            out_ref[1, a * b_count : (a + 1) * b_count, i * width : (i + 1) * width] = low


def core_kernel(q_ref, *refs):
    out_ref = refs[-1]
    pairs = refs[0].shape[0]
    rank = out_ref.shape[2]
    columns = [jnp.concatenate([r[p] for r in refs[:-1]], axis=0) for p in range(pairs)]
    high, low = split(jnp.concatenate(columns, axis=1))
    result = dot(q_ref[0], high) + (dot(q_ref[0], low) + dot(q_ref[1], high))
    for v in range(2 * pairs):
        out_ref[v] = result[:, v * HALF : v * HALF + rank]


def shifted(x, axis, count, k):
    return lax.ppermute(x, axis, [(i, (i + k) % count) for i in range(count)])


def gathered(x, axis):
    count = lax.axis_size(axis)
    if count <= 4:
        return [x] + [shifted(x, axis, count, k) for k in range(1, count)]
    blocks = lax.all_gather(x, axis)
    return [blocks[k] for k in range(count)]


def both_ways(low, high, axis):
    ends = lax.axis_size(axis) - 1
    from_low = lax.ppermute(high, axis, [(i, i + 1) for i in range(ends)])
    from_high = lax.ppermute(low, axis, [(i + 1, i) for i in range(ends)])
    return from_low, from_high


def beside(block, axis):
    if lax.axis_size(axis) == 2:
        return lax.ppermute(block, axis, [(0, 1), (1, 0)])
    from_low, from_high = both_ways(block, block, axis)
    row = lax.broadcasted_iota(jnp.int32, block.shape, 2)
    return jnp.where(row < REACH, from_high, from_low)


def local(fields, speeds, kinetics, block_rank, x_factor, y_factor, z_factor):
    nvars, nx, ny, nz = fields.shape
    rank = z_factor.shape[1]
    gx, gy, gz = (lax.axis_size(axis) for axis in ("gx", "gy", "gz"))
    iz = lax.axis_index("gz")
    rim = (nvars, REACH, ny, nz)
    plane = (nx, ny, nz)
    scratch = [pltpu.VMEM(fields.shape, F32), pltpu.VMEM(plane, F32)]

    low, high = call(
        rim_kernel,
        [(rim, F32), (rim, F32)],
        [pl.BlockSpec(memory_space=pl.ANY)],
        (fields,),
        [pltpu.SemaphoreType.DMA((2,))],
    )
    xl, xh = both_ways(low, high, "gx")
    (packed,) = call(pack_kernel, [(plane, F32)], [VMEM], (fields,))
    zl, zh = both_ways(packed, packed, "gz")
    other = beside(fields, "gy")
    ranks = gathered(block_rank.reshape(1, nx), "gx")
    y_rows = gathered(y_factor, "gy")
    weights, zf, dz, rim_shift, scales = call(
        weight_kernel,
        [
            ((2 * nvars * ny, 2 * nvars * ny), BF16),
            ((2 * nz, 4 * HALF), BF16),
            ((2 * nz, nz), BF16),
            ((nz, nz), BF16),
            ((nvars, 2, ny, nz), F32),
        ],
        [VMEM] * 3,
        (kinetics, speeds, z_factor.T),
        [pltpu.VMEM((nz, 2 * HALF), F32)],
    )
    section, low, high, packed = call(
        section_kernel,
        [(fields.shape, F32), (rim, F32), (rim, F32), (plane, F32)],
        [VMEM] * 10,
        (fields, xl, xh, other, zl, zh, weights, dz, rim_shift, scales),
        scratch,
    )
    low, high, packed, section, ranks, y_rows = lax.optimization_barrier((low, high, packed, section, ranks, y_rows))
    xl, xh = both_ways(low, high, "gx")
    zl, zh = both_ways(packed, packed, "gz")
    other = beside(section, "gy")
    a_count, b_count = x_factor.shape[1] // gx, y_factor.shape[1] // gy
    cells = gx * nx * gy * ny
    (factor,) = call(
        factor_kernel,
        [((2, a_count * b_count, cells), BF16)],
        [VMEM] * (2 + gy),
        (jnp.concatenate(ranks, axis=1), x_factor, *y_rows),
        [pltpu.VMEM((a_count, gx * nx * ny), F32)],
    )
    xl, xh, zl, zh, other, factor = lax.optimization_barrier((xl, xh, zl, zh, other, factor))
    fields_next, proj = call(
        next_kernel,
        [(fields.shape, F32), ((nvars // 2, nx * ny, 2 * HALF), F32)],
        [VMEM] * 12,
        (fields, section, xl, xh, other, zl, zh, weights, dz, rim_shift, zf, scales),
        scratch,
    )

    pairs = nvars // 2 // gz
    chunks = proj.reshape(gz, pairs, nx * ny, 2 * HALF)
    own = lax.dynamic_index_in_dim(chunks, iz, 0, keepdims=False)
    for k in range(1, gz):
        piece = lax.dynamic_index_in_dim(chunks, lax.rem(iz + k, gz), 0, keepdims=False)
        own = own + shifted(piece, "gz", gz, k)
    blocks = [gathered(block, "gy") for block in gathered(own, "gx")]
    parts = [blocks[i][j] for j in range(gy) for i in range(gx)]
    (core,) = call(
        core_kernel,
        [((2 * pairs, a_count * b_count, rank), F32)],
        [VMEM] * (1 + len(parts)),
        (factor, *parts),
        room=16 if cells <= 1024 else 50,
    )
    return fields_next, core.reshape(2 * pairs, a_count, b_count, rank)


def solution(mesh):
    placed = (P(None, "gx", "gy", "gz"), P(), P(), P("gx"), P(), P("gy", None), P("gz", None))
    return jax.shard_map(
        local,
        mesh=mesh,
        in_specs=placed,
        out_specs=(P(None, "gx", "gy", "gz"), P("gz", "gx", "gy", None)),
        check_vma=False,
    )
```

```python
import jax
import jax.numpy as jnp
from jax import lax
from jax.experimental import pallas as pl
from jax.experimental.pallas import tpu as pltpu
from jax.sharding import PartitionSpec as P

COEFFS = (0.8, -0.2, 4.0 / 105.0, -1.0 / 280.0)
SCALE = 840.0
WHOLE = (672.0, -168.0, 32.0, -3.0)
TIME_STEP = 0.45
REACH = len(COEFFS)
HALF = 64
F32, BF16 = jnp.float32, jnp.bfloat16
HIGHEST = lax.Precision.HIGHEST
VMEM = pl.BlockSpec(memory_space=pltpu.VMEM)
SMEM = pl.BlockSpec(memory_space=pltpu.SMEM)


def call(kernel, out_shapes, in_specs, args, scratch=(), room=16):
    return pl.pallas_call(
        kernel,
        out_shape=tuple(jax.ShapeDtypeStruct(s, d) for s, d in out_shapes),
        in_specs=in_specs,
        out_specs=tuple(VMEM for _ in out_shapes),
        scratch_shapes=list(scratch),
        compiler_params=pltpu.CompilerParams(vmem_limit_bytes=room * 2**20),
    )(*args)


def dot(a, b):
    return jnp.dot(a, b, preferred_element_type=F32)


def exact(a, b, dims=((1,), (0,))):
    return lax.dot_general(a, b, (dims, ((), ())), precision=HIGHEST, preferred_element_type=F32)


def split(x):
    high = x.astype(BF16)
    return high, (x - high.astype(F32)).astype(BF16)


def odd(axis):
    return lax.rem(lax.axis_index(axis), jnp.int32(2))


def rim_kernel(f_ref, first_ref, second_ref, sems):
    top, parity = f_ref.shape[1] - REACH, odd("gx")
    copies = [
        pltpu.make_async_copy(f_ref.at[:, pl.ds(start, REACH)], target, sems.at[i])
        for i, (start, target) in enumerate(((top * (1 - parity), first_ref), (top * parity, second_ref)))
    ]
    for copy in copies:
        copy.start()
    for copy in copies:
        copy.wait()


def pack_rim(v, values, rim_ref):
    width = values.shape[2]
    group = lax.shift_right_logical(lax.broadcasted_iota(jnp.int32, values.shape, 2), 2)
    last = pltpu.roll(values, REACH * v + REACH, 2)
    first = pltpu.roll(values, width // 2 + REACH * v, 2)
    rim = jnp.where(group == v, last, rim_ref[...])
    rim_ref[...] = jnp.where(group == v + width // 2 // REACH, first, rim)


def pack_kernel(f_ref, rim_ref, same_ref):
    rim_ref[...] = jnp.zeros_like(rim_ref)

    def step(v, carry):
        values = f_ref[v]
        same_ref[v] = values
        pack_rim(v, values, rim_ref)
        return carry

    lax.fori_loop(0, f_ref.shape[0], step, 0, unroll=4)


def iota(shape, dim):
    return lax.broadcasted_iota(jnp.int32, shape, dim)


def low_bits(x, size):
    return lax.rem(x, jnp.int32(size))


def weight_kernel(kin_ref, speed_ref, w_ref, dz_ref, shift_ref, scale_ref):
    nvars = kin_ref.shape[0]
    rows, columns = w_ref.shape[0] // 2, w_ref.shape[1]
    ny = rows // nvars
    spread = (iota((rows, nvars), 0) // ny == iota((rows, nvars), 1)).astype(F32)
    gather = (iota((nvars, columns), 1) // (2 * ny) == iota((nvars, columns), 0)).astype(F32)
    rates = exact(exact(spread, kin_ref[...]), gather)
    speed = exact(spread, speed_ref[...], ((1,), (1,)))[:, 1:2]
    row, column = iota((rows, columns), 0), iota((rows, columns), 1)
    y, other = low_bits(row, ny), low_bits(column, 2 * ny)
    iy = lax.axis_index("gy")
    below, above = iy > 0, iy < lax.axis_size("gy") - 1
    far = 8 * ny
    up = jnp.where(above, other - y, far)
    down = jnp.where(below, other - 2 * ny - y, far)
    offset = jnp.where(other < ny, other - y, jnp.where(other < ny + REACH, up, down))
    shifts = jnp.zeros((rows, columns), F32)
    for k in range(1, REACH + 1):
        shifts = jnp.where(offset == k, COEFFS[k - 1], jnp.where(offset == -k, -COEFFS[k - 1], shifts))
    shifts = jnp.where(row // ny == column // (2 * ny), speed * shifts, 0.0)
    high, low = split(TIME_STEP * (jnp.where(other == y, rates, 0.0) - shifts))
    w_ref[0:rows] = high
    w_ref[rows:] = low

    depth = dz_ref.shape[1]
    source, target = iota((depth, depth), 0), iota((depth, depth), 1)
    offset = source - target
    inner = jnp.zeros((depth, depth), F32)
    for k in range(1, REACH + 1):
        inner = jnp.where(offset == k, WHOLE[k - 1], jnp.where(offset == -k, -WHOLE[k - 1], inner))
    dz_ref[0:depth] = inner.astype(BF16)
    dz_ref[depth:] = inner.astype(BF16)
    turn = low_bits(target, REACH) - low_bits(source, REACH)
    first = source < depth // 2
    offset = REACH + jnp.where(first, turn, -turn)
    outer = jnp.zeros((depth, depth), F32)
    for k in range(1, REACH + 1):
        outer = jnp.where(offset == k, WHOLE[k - 1], outer)
    outer = jnp.where(source // REACH == target // REACH, jnp.where(first, -outer, outer), 0.0)
    shift_ref[...] = outer.astype(BF16)

    tile = scale_ref.shape[2:]
    for v in range(nvars):
        scale_ref[v, 0] = jnp.broadcast_to(TIME_STEP * speed_ref[0:1, v : v + 1], tile)
        scale_ref[v, 1] = jnp.broadcast_to(TIME_STEP / SCALE * speed_ref[2:3, v : v + 1], tile)


def project_kernel(zf_ref, zf_out_ref, wide_ref):
    depth, rank = zf_ref.shape[1], zf_ref.shape[0]
    identity = (iota((depth, depth), 0) == iota((depth, depth), 1)).astype(F32)
    wide_ref[...] = jnp.zeros_like(wide_ref)
    wide_ref[:, 0:rank] = exact(identity, zf_ref[...], ((1,), (1,)))
    high, low = split(wide_ref[...])
    zf_out_ref[0:depth, 0 : 2 * HALF] = high
    zf_out_ref[0:depth, 2 * HALF :] = low
    high, low = split(pltpu.roll(wide_ref[...], HALF, 1))
    zf_out_ref[depth:, 0 : 2 * HALF] = high
    zf_out_ref[depth:, 2 * HALF :] = low


def mix_planes(q_ref, beside_ref, w_ref, rate_ref):
    nvars, nx, ny, nz = q_ref.shape
    rows = nvars * ny

    def step(i, carry):
        high, low = [], []
        for p in (2 * i, 2 * i + 1):
            cells = jnp.concatenate([q_ref[:, p], beside_ref[:, p]], axis=1)
            h, l = split(cells.reshape(2 * rows, nz))
            high.append(h)
            low.append(l)
        both = dot(w_ref[...], jnp.concatenate(high, axis=1))
        total = both[:rows] + both[rows:] + dot(w_ref[0:rows], jnp.concatenate(low, axis=1))
        for j in range(2):
            rate_ref[:, 2 * i + j] = total[:, j * nz : (j + 1) * nz].reshape(nvars, ny, nz)
        return carry

    lax.fori_loop(0, nx // 2, step, 0, unroll=True)


def join_rims(first_ref, second_ref, shift_ref, rim_ref):
    nx, ny, nz = rim_ref.shape
    upper = lax.shift_right_logical(iota(rim_ref.shape, 2) * 2 // nz, 0)
    rim = jnp.where(upper == odd("gz"), second_ref[...], first_ref[...]).reshape(nx * ny, nz)
    high, low = split(rim)
    rim_ref[...] = (dot(high, shift_ref[...]) + dot(low, shift_ref[...])).reshape(rim_ref.shape)


def step_of(v, q_ref, first_ref, second_ref, dz_ref, rate_ref, rim_ref, scale_ref):
    _, nx, ny, nz = q_ref.shape
    q = q_ref[v]
    even = jnp.full((REACH, ny, nz), odd("gx")) == 0
    low_rim = jnp.where(even, second_ref[v], first_ref[v])
    high_rim = jnp.where(even, first_ref[v], second_ref[v])
    tall = jnp.concatenate([low_rim, q, high_rim], axis=0)
    gx = None
    for k in range(1, REACH + 1):
        part = COEFFS[k - 1] * (tall[REACH + k : REACH + k + nx] - tall[REACH - k : REACH - k + nx])
        gx = part if gx is None else gx + part
    high, low = split(q.reshape(nx * ny, nz))
    gz = dot(jnp.concatenate([high, low], axis=1), dz_ref[...]).reshape(nx, ny, nz)
    lane = lax.broadcasted_iota(jnp.int32, q.shape, 2)
    rim = rim_ref[...]
    first = pltpu.roll(rim, lax.rem(nz - REACH * v, nz), 2)
    last = pltpu.roll(rim, nz // 2 - REACH - REACH * v, 2)
    gz = gz + jnp.where(lane < REACH, first, jnp.where(lane >= nz - REACH, last, 0.0))
    return rate_ref[v] - scale_ref[v, 0] * gx - scale_ref[v, 1] * gz


def section_kernel(
    f_ref, x1_ref, x2_ref, beside_ref, z1_ref, z2_ref, w_ref, dz_ref, shift_ref, scale_ref,
    s_ref, first_ref, second_ref, out_rim_ref, rate_ref, rim_ref,
):
    mix_planes(f_ref, beside_ref, w_ref, rate_ref)
    join_rims(z1_ref, z2_ref, shift_ref, rim_ref)
    out_rim_ref[...] = jnp.zeros_like(out_rim_ref)

    def step(v, carry):
        s = f_ref[v] + step_of(v, f_ref, x1_ref, x2_ref, dz_ref, rate_ref, rim_ref, scale_ref)
        s_ref[v] = s
        low, high = s[:REACH], s[s.shape[0] - REACH :]
        even = jnp.full(low.shape, odd("gx")) == 0
        first_ref[v] = jnp.where(even, high, low)
        second_ref[v] = jnp.where(even, low, high)
        pack_rim(v, s, out_rim_ref)
        return carry

    lax.fori_loop(0, f_ref.shape[0], step, 0, unroll=4)


def next_kernel(
    f_ref, s_ref, x1_ref, x2_ref, beside_ref, z1_ref, z2_ref, w_ref, dz_ref, shift_ref, scale_ref, zf_ref,
    next_ref, *refs,
):
    _, nx, ny, nz = f_ref.shape
    chunk_refs, (rate_ref, rim_ref) = refs[:-2], refs[-2:]
    mix_planes(s_ref, beside_ref, w_ref, rate_ref)
    join_rims(z1_ref, z2_ref, shift_ref, rim_ref)
    count, pairs = len(chunk_refs), chunk_refs[0].shape[0]
    for k, chunk_ref in enumerate(chunk_refs):
        start = lax.rem(lax.axis_index("gz") + k, jnp.int32(count)) * (2 * pairs)
        for j in range(pairs):
            both = []
            for v in (start + 2 * j, start + 2 * j + 1):
                rate = step_of(v, s_ref, x1_ref, x2_ref, dz_ref, rate_ref, rim_ref, scale_ref)
                new = 0.5 * (f_ref[v] + s_ref[v] + rate)
                next_ref[v] = new
                both.append(new.reshape(nx * ny, nz))
            high, low = split(jnp.concatenate(both, axis=1))
            wide = dot(high, zf_ref[...])
            chunk_ref[j] = wide[:, : 2 * HALF] + wide[:, 2 * HALF :] + dot(low, zf_ref[:, : 2 * HALF])


def sum_kernel(*refs):
    total = refs[0][...]
    for ref in refs[1:-1]:
        total = total + ref[...]
    refs[-1][...] = total


def factor_kernel(rank_ref, xf_ref, *refs):
    y_refs, (out_ref, xt_ref) = refs[:-2], refs[-2:]
    planes, a_count = rank_ref.shape[1], xt_ref.shape[0]
    ny = y_refs[0].shape[0]
    width = planes * ny
    b_count = out_ref.shape[1] // a_count

    def own(count, total, place):
        column = lax.broadcasted_iota(jnp.int32, (count, total), 1)
        return (column == lax.broadcasted_iota(jnp.int32, (count, total), 0) + place * count).astype(F32)

    mine = exact(own(a_count, xf_ref.shape[1], lax.axis_index("gx")), xf_ref[...], ((1,), (1,)))
    pick = lax.broadcasted_iota(jnp.int32, (xf_ref.shape[0], planes), 0) == rank_ref[...]
    mine = exact(mine, pick.astype(F32))
    column = lax.broadcasted_iota(jnp.int32, (planes, width), 1)
    spread = lax.broadcasted_iota(jnp.int32, (planes, width), 0) == column // ny
    xt_ref[...] = exact(mine, spread.astype(F32))
    column = lax.broadcasted_iota(jnp.int32, (ny, width), 1)
    spread = lax.broadcasted_iota(jnp.int32, (ny, width), 0) == lax.rem(column, ny)
    for i, y_ref in enumerate(y_refs):
        rows = exact(own(b_count, y_ref.shape[1], lax.axis_index("gy")), y_ref[...], ((1,), (1,)))
        yt = exact(rows, spread.astype(F32))
        for a in range(a_count):
            high, low = split(xt_ref[a : a + 1, :] * yt)
            out_ref[0, a * b_count : (a + 1) * b_count, i * width : (i + 1) * width] = high
            out_ref[1, a * b_count : (a + 1) * b_count, i * width : (i + 1) * width] = low


def core_kernel(q_ref, *refs):
    out_ref = refs[-1]
    pairs = refs[0].shape[0]
    rank = out_ref.shape[2]
    columns = [jnp.concatenate([r[p] for r in refs[:-1]], axis=0) for p in range(pairs)]
    high, low = split(jnp.concatenate(columns, axis=1))
    result = dot(q_ref[0], high) + (dot(q_ref[0], low) + dot(q_ref[1], high))
    for v in range(2 * pairs):
        out_ref[v] = result[:, v * HALF : v * HALF + rank]


def shifted(x, axis, k):
    count = lax.axis_size(axis)
    return lax.ppermute(x, axis, [(i, (i + k) % count) for i in range(count)])


def gathered(x, axis):
    count = lax.axis_size(axis)
    if count <= 4:
        return [x] + [shifted(x, axis, k) for k in range(1, count)]
    blocks = lax.all_gather(x, axis)
    return [blocks[k] for k in range(count)]


def paired(first, second, axis):
    out = []
    for x, start in ((first, 0), (second, 1)):
        links = [(i, i + 1) for i in range(start, lax.axis_size(axis) - 1, 2)]
        out.append(lax.ppermute(x, axis, links + [(j, i) for i, j in links]))
    return out


def beside(block, axis):
    count = lax.axis_size(axis)
    if count == 2:
        return lax.ppermute(block, axis, [(0, 1), (1, 0)])
    from_low = lax.ppermute(block, axis, [(i, i + 1) for i in range(count - 1)])
    from_high = lax.ppermute(block, axis, [(i + 1, i) for i in range(count - 1)])
    row = lax.broadcasted_iota(jnp.int32, block.shape, 2)
    return jnp.where(row < REACH, from_high, from_low)


def local(fields, speeds, kinetics, block_rank, x_factor, y_factor, z_factor):
    nvars, nx, ny, nz = fields.shape
    rank = z_factor.shape[1]
    gx, gy, gz = (lax.axis_size(axis) for axis in ("gx", "gy", "gz"))
    rim = (nvars, REACH, ny, nz)
    plane = (nx, ny, nz)
    scratch = [pltpu.VMEM(fields.shape, F32), pltpu.VMEM(plane, F32)]
    pairs = nvars // 2 // gz
    chunk = (pairs, nx * ny, 2 * HALF)
    barrier = lax.optimization_barrier

    first, second = call(
        rim_kernel,
        [(rim, F32), (rim, F32)],
        [pl.BlockSpec(memory_space=pltpu.HBM)],
        (fields,),
        [pltpu.SemaphoreType.DMA((2,))],
    )
    x1, x2 = paired(first, second, "gx")
    packed, same = call(pack_kernel, [(plane, F32), (fields.shape, F32)], [VMEM], (fields,))
    z1, z2 = paired(packed, packed, "gz")
    other = beside(fields, "gy")
    weights, dz, rim_shift, scales = call(
        weight_kernel,
        [((2 * nvars * ny, 2 * nvars * ny), BF16), ((2 * nz, nz), BF16), ((nz, nz), BF16), ((nvars, 2, ny, nz), F32)],
        [VMEM] * 2,
        (kinetics, speeds),
    )
    section, first, second, packed = call(
        section_kernel,
        [(fields.shape, F32), (rim, F32), (rim, F32), (plane, F32)],
        [VMEM] * 10,
        (same, x1, x2, other, z1, z2, weights, dz, rim_shift, scales),
        scratch,
    )
    section, first, second, packed, z_factor = barrier((section, first, second, packed, z_factor))
    x1, x2 = paired(first, second, "gx")
    z1, z2 = paired(packed, packed, "gz")
    other = beside(section, "gy")
    (zf,) = call(project_kernel, [((2 * nz, 4 * HALF), BF16)], [VMEM], (z_factor.T,), [pltpu.VMEM((nz, 2 * HALF), F32)])
    fields_next, *chunks = call(
        next_kernel,
        [(fields.shape, F32)] + [(chunk, F32)] * gz,
        [VMEM] * 12,
        (fields, section, x1, x2, other, z1, z2, weights, dz, rim_shift, scales, zf),
        scratch,
    )
    chunks, block_rank, y_factor = barrier((chunks, block_rank, y_factor))
    parts = [chunks[0]] + [shifted(chunks[k], "gz", k) for k in range(1, gz)]
    ranks = gathered(block_rank.reshape(1, nx), "gx")
    y_rows = gathered(y_factor, "gy")
    (own,) = call(sum_kernel, [(chunk, F32)], [VMEM] * gz, parts)
    a_count, b_count = x_factor.shape[1] // gx, y_factor.shape[1] // gy
    cells = gx * nx * gy * ny
    (factor,) = call(
        factor_kernel,
        [((2, a_count * b_count, cells), BF16)],
        [VMEM] * (2 + gy),
        (jnp.concatenate(ranks, axis=1), x_factor, *y_rows),
        [pltpu.VMEM((a_count, gx * nx * ny), F32)],
    )
    blocks = [gathered(block, "gy") for block in gathered(own, "gx")]
    parts = [blocks[i][j] for j in range(gy) for i in range(gx)]
    (core,) = call(
        core_kernel,
        [((2 * pairs, a_count * b_count, rank), F32)],
        [VMEM] * (1 + len(parts)),
        (factor, *parts),
        room=16 if cells <= 1024 else 50,
    )
    return fields_next, core.reshape(2 * pairs, a_count, b_count, rank)


def solution(mesh):
    placed = (P(None, "gx", "gy", "gz"), P(), P(), P("gx"), P(), P("gy", None), P("gz", None))
    return jax.shard_map(
        local,
        mesh=mesh,
        in_specs=placed,
        out_specs=(P(None, "gx", "gy", "gz"), P("gz", "gx", "gy", None)),
        check_vma=False,
    )
```

```python
import jax
import jax.numpy as jnp
from jax import lax
from jax.experimental import pallas as pl
from jax.experimental.pallas import tpu as pltpu
from jax.sharding import PartitionSpec as P

COEFFS = (0.8, -0.2, 4.0 / 105.0, -1.0 / 280.0)
SCALE = 840.0
WHOLE = (672.0, -168.0, 32.0, -3.0)
TIME_STEP = 0.45
REACH = len(COEFFS)
HALF = 64
F32, BF16 = jnp.float32, jnp.bfloat16
HIGHEST = lax.Precision.HIGHEST
VMEM = pl.BlockSpec(memory_space=pltpu.VMEM)
SMEM = pl.BlockSpec(memory_space=pltpu.SMEM)
ANY = pl.BlockSpec(memory_space=pl.ANY)
HBM = pl.BlockSpec(memory_space=pltpu.HBM)


def call(kernel, out_shapes, in_specs, args, scratch=(), room=16, out_spec=VMEM):
    return pl.pallas_call(
        kernel,
        out_shape=tuple(jax.ShapeDtypeStruct(s, d) for s, d in out_shapes),
        in_specs=in_specs,
        out_specs=tuple(out_spec for _ in out_shapes),
        scratch_shapes=list(scratch),
        compiler_params=pltpu.CompilerParams(vmem_limit_bytes=room * 2**20),
    )(*args)


def dot(a, b):
    return jnp.dot(a, b, preferred_element_type=F32)


def exact(a, b, dims=((1,), (0,))):
    return lax.dot_general(a, b, (dims, ((), ())), precision=HIGHEST, preferred_element_type=F32)


def split(x):
    high = x.astype(BF16)
    return high, (x - high.astype(F32)).astype(BF16)


def odd(axis):
    return lax.rem(lax.axis_index(axis), jnp.int32(2))


def rim_kernel(f_ref, first_ref, second_ref, sems):
    top, parity = f_ref.shape[1] - REACH, odd("gx")
    copies = [
        pltpu.make_async_copy(f_ref.at[:, pl.ds(start, REACH)], target, sems.at[i])
        for i, (start, target) in enumerate(((top * (1 - parity), first_ref), (top * parity, second_ref)))
    ]
    for copy in copies:
        copy.start()
    for copy in copies:
        copy.wait()


def pack_rim(v, values, rim_ref):
    width = values.shape[2]
    group = lax.shift_right_logical(lax.broadcasted_iota(jnp.int32, values.shape, 2), 2)
    last = pltpu.roll(values, REACH * v + REACH, 2)
    first = pltpu.roll(values, width // 2 + REACH * v, 2)
    rim = jnp.where(group == v, last, rim_ref[...])
    rim_ref[...] = jnp.where(group == v + width // 2 // REACH, first, rim)


def pack_kernel(f_ref, rim_ref, same_ref):
    rim_ref[...] = jnp.zeros_like(rim_ref)

    def step(v, carry):
        values = f_ref[v]
        same_ref[v] = values
        pack_rim(v, values, rim_ref)
        return carry

    lax.fori_loop(0, f_ref.shape[0], step, 0, unroll=4)


def iota(shape, dim):
    return lax.broadcasted_iota(jnp.int32, shape, dim)


def low_bits(x, size):
    return lax.rem(x, jnp.int32(size))


def weight_kernel(kin_ref, speed_ref, w_ref, dz_ref, shift_ref, scale_ref):
    nvars = kin_ref.shape[0]
    rows, columns = w_ref.shape[0] // 2, w_ref.shape[1]
    ny = rows // nvars
    spread = (iota((rows, nvars), 0) // ny == iota((rows, nvars), 1)).astype(F32)
    gather = (iota((nvars, columns), 1) // (2 * ny) == iota((nvars, columns), 0)).astype(F32)
    rates = exact(exact(spread, kin_ref[...]), gather)
    speed = exact(spread, speed_ref[...], ((1,), (1,)))[:, 1:2]
    row, column = iota((rows, columns), 0), iota((rows, columns), 1)
    y, other = low_bits(row, ny), low_bits(column, 2 * ny)
    iy = lax.axis_index("gy")
    below, above = iy > 0, iy < lax.axis_size("gy") - 1
    far = 8 * ny
    up = jnp.where(above, other - y, far)
    down = jnp.where(below, other - 2 * ny - y, far)
    offset = jnp.where(other < ny, other - y, jnp.where(other < ny + REACH, up, down))
    shifts = jnp.zeros((rows, columns), F32)
    for k in range(1, REACH + 1):
        shifts = jnp.where(offset == k, COEFFS[k - 1], jnp.where(offset == -k, -COEFFS[k - 1], shifts))
    shifts = jnp.where(row // ny == column // (2 * ny), speed * shifts, 0.0)
    high, low = split(TIME_STEP * (jnp.where(other == y, rates, 0.0) - shifts))
    w_ref[0:rows] = high
    w_ref[rows:] = low

    depth = dz_ref.shape[1]
    source, target = iota((depth, depth), 0), iota((depth, depth), 1)
    offset = source - target
    inner = jnp.zeros((depth, depth), F32)
    for k in range(1, REACH + 1):
        inner = jnp.where(offset == k, WHOLE[k - 1], jnp.where(offset == -k, -WHOLE[k - 1], inner))
    dz_ref[0:depth] = inner.astype(BF16)
    dz_ref[depth:] = inner.astype(BF16)
    turn = low_bits(target, REACH) - low_bits(source, REACH)
    first = source < depth // 2
    offset = REACH + jnp.where(first, turn, -turn)
    outer = jnp.zeros((depth, depth), F32)
    for k in range(1, REACH + 1):
        outer = jnp.where(offset == k, WHOLE[k - 1], outer)
    outer = jnp.where(source // REACH == target // REACH, jnp.where(first, -outer, outer), 0.0)
    shift_ref[...] = outer.astype(BF16)

    tile = scale_ref.shape[2:]
    for v in range(nvars):
        scale_ref[v, 0] = jnp.broadcast_to(TIME_STEP * speed_ref[0:1, v : v + 1], tile)
        scale_ref[v, 1] = jnp.broadcast_to(TIME_STEP / SCALE * speed_ref[2:3, v : v + 1], tile)


def project_kernel(zf_ref, zf_out_ref, wide_ref):
    depth, rank = zf_ref.shape[1], zf_ref.shape[0]
    identity = (iota((depth, depth), 0) == iota((depth, depth), 1)).astype(F32)
    wide_ref[...] = jnp.zeros_like(wide_ref)
    wide_ref[:, 0:rank] = exact(identity, zf_ref[...], ((1,), (1,)))
    high, low = split(wide_ref[...])
    zf_out_ref[0:depth, 0 : 2 * HALF] = high
    zf_out_ref[0:depth, 2 * HALF :] = low
    high, low = split(pltpu.roll(wide_ref[...], HALF, 1))
    zf_out_ref[depth:, 0 : 2 * HALF] = high
    zf_out_ref[depth:, 2 * HALF :] = low


def mix_planes(q_ref, beside_ref, w_ref, rate_ref):
    nvars, nx, ny, nz = q_ref.shape
    rows = nvars * ny

    def step(i, carry):
        high, low = [], []
        for p in (2 * i, 2 * i + 1):
            cells = jnp.concatenate([q_ref[:, p], beside_ref[:, p]], axis=1)
            h, l = split(cells.reshape(2 * rows, nz))
            high.append(h)
            low.append(l)
        both = dot(w_ref[...], jnp.concatenate(high, axis=1))
        total = both[:rows] + both[rows:] + dot(w_ref[0:rows], jnp.concatenate(low, axis=1))
        for j in range(2):
            rate_ref[:, 2 * i + j] = total[:, j * nz : (j + 1) * nz].reshape(nvars, ny, nz)
        return carry

    lax.fori_loop(0, nx // 2, step, 0, unroll=True)


def join_rims(first_ref, second_ref, shift_ref, rim_ref):
    nx, ny, nz = rim_ref.shape
    upper = lax.shift_right_logical(iota(rim_ref.shape, 2) * 2 // nz, 0)
    rim = jnp.where(upper == odd("gz"), second_ref[...], first_ref[...]).reshape(nx * ny, nz)
    high, low = split(rim)
    rim_ref[...] = (dot(high, shift_ref[...]) + dot(low, shift_ref[...])).reshape(rim_ref.shape)


def step_of(v, q_ref, first_ref, second_ref, dz_ref, rate_ref, rim_ref, scale_ref):
    _, nx, ny, nz = q_ref.shape
    q = q_ref[v]
    even = jnp.full((REACH, ny, nz), odd("gx")) == 0
    low_rim = jnp.where(even, second_ref[v], first_ref[v])
    high_rim = jnp.where(even, first_ref[v], second_ref[v])
    tall = jnp.concatenate([low_rim, q, high_rim], axis=0)
    gx = None
    for k in range(1, REACH + 1):
        part = COEFFS[k - 1] * (tall[REACH + k : REACH + k + nx] - tall[REACH - k : REACH - k + nx])
        gx = part if gx is None else gx + part
    high, low = split(q.reshape(nx * ny, nz))
    gz = dot(jnp.concatenate([high, low], axis=1), dz_ref[...]).reshape(nx, ny, nz)
    lane = lax.broadcasted_iota(jnp.int32, q.shape, 2)
    rim = rim_ref[...]
    first = pltpu.roll(rim, lax.rem(nz - REACH * v, nz), 2)
    last = pltpu.roll(rim, nz // 2 - REACH - REACH * v, 2)
    gz = gz + jnp.where(lane < REACH, first, jnp.where(lane >= nz - REACH, last, 0.0))
    return rate_ref[v] - scale_ref[v, 0] * gx - scale_ref[v, 1] * gz


def section_kernel(
    f_ref, x1_ref, x2_ref, beside_ref, z1_ref, z2_ref, w_ref, dz_ref, shift_ref, scale_ref,
    s_ref, first_ref, second_ref, out_rim_ref, rate_ref, rim_ref,
):
    mix_planes(f_ref, beside_ref, w_ref, rate_ref)
    join_rims(z1_ref, z2_ref, shift_ref, rim_ref)
    out_rim_ref[...] = jnp.zeros_like(out_rim_ref)

    def step(v, carry):
        s = f_ref[v] + step_of(v, f_ref, x1_ref, x2_ref, dz_ref, rate_ref, rim_ref, scale_ref)
        s_ref[v] = s
        low, high = s[:REACH], s[s.shape[0] - REACH :]
        even = jnp.full(low.shape, odd("gx")) == 0
        first_ref[v] = jnp.where(even, high, low)
        second_ref[v] = jnp.where(even, low, high)
        pack_rim(v, s, out_rim_ref)
        return carry

    lax.fori_loop(0, f_ref.shape[0], step, 0, unroll=4)


def next_kernel(
    f_ref, s_ref, x1_ref, x2_ref, beside_ref, z1_ref, z2_ref, w_ref, dz_ref, shift_ref, scale_ref, zf_ref,
    next_ref, *refs,
):
    _, nx, ny, nz = f_ref.shape
    chunk_refs, (rate_ref, rim_ref) = refs[:-2], refs[-2:]
    mix_planes(s_ref, beside_ref, w_ref, rate_ref)
    join_rims(z1_ref, z2_ref, shift_ref, rim_ref)
    count, pairs = len(chunk_refs), chunk_refs[0].shape[0]
    for k, chunk_ref in enumerate(chunk_refs):
        start = lax.rem(lax.axis_index("gz") + k, jnp.int32(count)) * (2 * pairs)
        for j in range(pairs):
            both = []
            for v in (start + 2 * j, start + 2 * j + 1):
                rate = step_of(v, s_ref, x1_ref, x2_ref, dz_ref, rate_ref, rim_ref, scale_ref)
                new = 0.5 * (f_ref[v] + s_ref[v] + rate)
                next_ref[v] = new
                both.append(new.reshape(nx * ny, nz))
            high, low = split(jnp.concatenate(both, axis=1))
            wide = dot(high, zf_ref[...])
            chunk_ref[j] = wide[:, : 2 * HALF] + wide[:, 2 * HALF :] + dot(low, zf_ref[:, : 2 * HALF])


def sum_kernel(*refs):
    total = refs[0][...]
    for ref in refs[1:-1]:
        total = total + ref[...]
    refs[-1][...] = total


def store_kernel(in_ref, out_ref, sem):
    copy = pltpu.make_async_copy(in_ref, out_ref, sem)
    copy.start()
    copy.wait()


def factor_kernel(xf_ref, *refs):
    y_refs, (out_ref, xt_ref) = refs[:-2], refs[-2:]
    planes, a_count = xf_ref.shape[0], xt_ref.shape[0]
    ny = y_refs[0].shape[0]
    width = planes * ny
    b_count = out_ref.shape[1] // a_count

    def own(count, total, place):
        return (iota((count, total), 1) == iota((count, total), 0) + place * count).astype(F32)

    mine = exact(own(a_count, xf_ref.shape[1], lax.axis_index("gx")), xf_ref[...], ((1,), (1,)))
    spread = iota((planes, width), 0) == iota((planes, width), 1) // ny
    xt_ref[...] = exact(mine, spread.astype(F32))
    spread = iota((ny, width), 0) == low_bits(iota((ny, width), 1), ny)
    for i, y_ref in enumerate(y_refs):
        rows = exact(own(b_count, y_ref.shape[1], lax.axis_index("gy")), y_ref[...], ((1,), (1,)))
        yt = exact(rows, spread.astype(F32))
        for a in range(a_count):
            high, low = split(xt_ref[a : a + 1, :] * yt)
            out_ref[0, a * b_count : (a + 1) * b_count, i * width : (i + 1) * width] = high
            out_ref[1, a * b_count : (a + 1) * b_count, i * width : (i + 1) * width] = low


def core_kernel(rank_ref, q_ref, *refs):
    block_refs, (out_ref, placed_ref, result_ref, sems) = refs[:-4], refs[-4:]
    pairs, blocks_y, planes, ny, nz = placed_ref.shape
    nx = block_refs[0].shape[1] // ny
    rank = out_ref.shape[2]
    rows = out_ref.shape[1] // sems.shape[0]
    for i in range(planes // nx):
        for x in range(nx):
            row = rank_ref[i * nx + x]
            for j in range(blocks_y):
                for p in range(pairs):
                    block_ref = block_refs[i * blocks_y + j]
                    placed_ref[p, j, row] = block_ref[p, x * ny : (x + 1) * ny, :]
    columns = [placed_ref[p].reshape(blocks_y * planes * ny, nz) for p in range(pairs)]
    high, low = split(jnp.concatenate(columns, axis=1))
    copies = []
    for m in range(sems.shape[0]):
        here = slice(m * rows, (m + 1) * rows)
        q_high = q_ref[0, here]
        result = dot(q_high, high) + (dot(q_high, low) + dot(q_ref[1, here], high))
        for v in range(2 * pairs):
            result_ref[v, here] = result[:, v * HALF : v * HALF + rank]
        copies.append(pltpu.make_async_copy(result_ref.at[:, here], out_ref.at[:, here], sems.at[m]))
        copies[-1].start()
    for copy in copies:
        copy.wait()


def shifted(x, axis, k):
    count = lax.axis_size(axis)
    return lax.ppermute(x, axis, [(i, (i + k) % count) for i in range(count)])


def gathered(x, axis):
    count = lax.axis_size(axis)
    if count <= 4:
        return [x] + [shifted(x, axis, k) for k in range(1, count)]
    blocks = lax.all_gather(x, axis)
    return [blocks[k] for k in range(count)]


def gathered_on_chip(x):
    count = lax.axis_size("gx")
    if count != 4 or lax.axis_size("gy") != 2:
        return gathered(x, "gx")
    ring = [((i, j), ((i + (1, 3)[j]) % 4, j)) for i in range(4) for j in range(2)]
    mine = lax.ppermute(x, ("gx", "gy"), [(2 * i + j, 2 * k + l) for (i, j), (k, l) in ring])
    across = shifted(x, "gx", 2)
    theirs = lax.ppermute(mine, "gy", [(0, 1), (1, 0)])
    upper = lax.axis_index("gy") == 1
    return [x, jnp.where(upper, theirs, mine), across, jnp.where(upper, mine, theirs)]


def paired(first, second, axis):
    out = []
    for x, start in ((first, 0), (second, 1)):
        links = [(i, i + 1) for i in range(start, lax.axis_size(axis) - 1, 2)]
        out.append(lax.ppermute(x, axis, links + [(j, i) for i, j in links]))
    return out


def beside(block, axis):
    count = lax.axis_size(axis)
    if count == 2:
        return lax.ppermute(block, axis, [(0, 1), (1, 0)])
    from_low = lax.ppermute(block, axis, [(i, i + 1) for i in range(count - 1)])
    from_high = lax.ppermute(block, axis, [(i + 1, i) for i in range(count - 1)])
    row = lax.broadcasted_iota(jnp.int32, block.shape, 2)
    return jnp.where(row < REACH, from_high, from_low)


def local(fields, speeds, kinetics, block_rank, x_factor, y_factor, z_factor):
    nvars, nx, ny, nz = fields.shape
    rank = z_factor.shape[1]
    gx, gy, gz = (lax.axis_size(axis) for axis in ("gx", "gy", "gz"))
    rim = (nvars, REACH, ny, nz)
    plane = (nx, ny, nz)
    scratch = [pltpu.VMEM(fields.shape, F32), pltpu.VMEM(plane, F32)]
    pairs = nvars // 2 // gz
    chunk = (pairs, nx * ny, 2 * HALF)
    barrier = lax.optimization_barrier

    first, second = call(
        rim_kernel,
        [(rim, F32), (rim, F32)],
        [HBM],
        (fields,),
        [pltpu.SemaphoreType.DMA((2,))],
    )
    x1, x2 = paired(first, second, "gx")
    packed, same = call(pack_kernel, [(plane, F32), (fields.shape, F32)], [VMEM], (fields,))
    z1, z2 = paired(packed, packed, "gz")
    other = beside(fields, "gy")
    weights, dz, rim_shift, scales = call(
        weight_kernel,
        [((2 * nvars * ny, 2 * nvars * ny), BF16), ((2 * nz, nz), BF16), ((nz, nz), BF16), ((nvars, 2, ny, nz), F32)],
        [VMEM] * 2,
        (kinetics, speeds),
    )
    section, first, second, packed = call(
        section_kernel,
        [(fields.shape, F32), (rim, F32), (rim, F32), (plane, F32)],
        [VMEM] * 10,
        (same, x1, x2, other, z1, z2, weights, dz, rim_shift, scales),
        scratch,
    )
    a_count, b_count = x_factor.shape[1] // gx, y_factor.shape[1] // gy
    rows, planes = a_count * b_count, gx * nx
    cells = planes * gy * ny
    section, first, second, packed, z_factor, x_factor, y_factor = barrier(
        (section, first, second, packed, z_factor, x_factor, y_factor)
    )
    x1, x2 = paired(first, second, "gx")
    z1, z2 = paired(packed, packed, "gz")
    other = beside(section, "gy")
    y_rows = gathered(y_factor, "gy")
    (zf,) = call(project_kernel, [((2 * nz, 4 * HALF), BF16)], [VMEM], (z_factor.T,), [pltpu.VMEM((nz, 2 * HALF), F32)])
    (factor,) = call(
        factor_kernel,
        [((2, rows, cells), BF16)],
        [VMEM] * (1 + gy),
        (x_factor, *y_rows),
        [pltpu.VMEM((a_count, planes * ny), F32)],
    )
    x1, x2, z1, z2, other, zf, factor = barrier((x1, x2, z1, z2, other, zf, factor))
    new, *chunks = call(
        next_kernel,
        [(fields.shape, F32)] + [(chunk, F32)] * gz,
        [VMEM] * 12,
        (fields, section, x1, x2, other, z1, z2, weights, dz, rim_shift, scales, zf),
        scratch,
    )
    new, chunks, block_rank = barrier((new, chunks, block_rank))
    parts = [chunks[0]] + [shifted(chunks[k], "gz", k) for k in range(1, gz)]
    ranks = jnp.concatenate(gathered_on_chip(block_rank), axis=0)
    (fields_next,) = call(store_kernel, [(fields.shape, F32)], [ANY], (new,), [pltpu.SemaphoreType.DMA], out_spec=HBM)
    (own,) = call(sum_kernel, [(chunk, F32)], [VMEM] * gz, parts)
    blocks = [gathered(block, "gy") for block in gathered(own, "gx")]
    pieces = 4 if rows % 128 == 0 else 1
    (core,) = call(
        core_kernel,
        [((2 * pairs, rows, rank), F32)],
        [SMEM] + [VMEM] * (1 + gx * gy),
        (ranks, factor, *(block for line in blocks for block in line)),
        [
            pltpu.VMEM((pairs, gy, planes, ny, nz), F32),
            pltpu.VMEM((2 * pairs, rows, rank), F32),
            pltpu.SemaphoreType.DMA((pieces,)),
        ],
        room=16 if cells <= 1024 else 56,
        out_spec=HBM,
    )
    return fields_next, core.reshape(2 * pairs, a_count, b_count, rank)


def solution(mesh):
    placed = (P(None, "gx", "gy", "gz"), P(), P(), P("gx"), P(), P("gy", None), P("gz", None))
    return jax.shard_map(
        local,
        mesh=mesh,
        in_specs=placed,
        out_specs=(P(None, "gx", "gy", "gz"), P("gz", "gx", "gy", None)),
        check_vma=False,
    )
```

```python
import jax
import jax.numpy as jnp
from jax import lax
from jax.experimental import pallas as pl
from jax.experimental.pallas import tpu as pltpu
from jax.sharding import PartitionSpec as P

COEFFS = (0.8, -0.2, 4.0 / 105.0, -1.0 / 280.0)
SCALE = 840.0
WHOLE = (672.0, -168.0, 32.0, -3.0)
TIME_STEP = 0.45
REACH = len(COEFFS)
HALF = 64
F32, BF16 = jnp.float32, jnp.bfloat16
HIGHEST = lax.Precision.HIGHEST
VMEM = pl.BlockSpec(memory_space=pltpu.VMEM)
SMEM = pl.BlockSpec(memory_space=pltpu.SMEM)
ANY = pl.BlockSpec(memory_space=pl.ANY)
HBM = pl.BlockSpec(memory_space=pltpu.HBM)


def call(kernel, out_shapes, in_specs, args, scratch=(), room=16, out_spec=VMEM):
    return pl.pallas_call(
        kernel,
        out_shape=tuple(jax.ShapeDtypeStruct(s, d) for s, d in out_shapes),
        in_specs=in_specs,
        out_specs=tuple(out_spec for _ in out_shapes),
        scratch_shapes=list(scratch),
        compiler_params=pltpu.CompilerParams(vmem_limit_bytes=room * 2**20),
    )(*args)


def dot(a, b):
    return jnp.dot(a, b, preferred_element_type=F32)


def exact(a, b, dims=((1,), (0,))):
    return lax.dot_general(a, b, (dims, ((), ())), precision=HIGHEST, preferred_element_type=F32)


def split(x):
    high = x.astype(BF16)
    return high, (x - high.astype(F32)).astype(BF16)


def odd(axis):
    return lax.rem(lax.axis_index(axis), jnp.int32(2))


def rim_kernel(f_ref, first_ref, second_ref, sems):
    top, parity = f_ref.shape[1] - REACH, odd("gx")
    copies = [
        pltpu.make_async_copy(f_ref.at[:, pl.ds(start, REACH)], target, sems.at[i])
        for i, (start, target) in enumerate(((top * (1 - parity), first_ref), (top * parity, second_ref)))
    ]
    for copy in copies:
        copy.start()
    for copy in copies:
        copy.wait()


def pack_rim(v, values, rim_ref):
    width = values.shape[2]
    group = lax.shift_right_logical(lax.broadcasted_iota(jnp.int32, values.shape, 2), 2)
    last = pltpu.roll(values, REACH * v + REACH, 2)
    first = pltpu.roll(values, width // 2 + REACH * v, 2)
    rim = jnp.where(group == v, last, rim_ref[...])
    rim_ref[...] = jnp.where(group == v + width // 2 // REACH, first, rim)


def pack_kernel(f_ref, rim_ref, same_ref, sems):
    count = f_ref.shape[0] // sems.shape[0]
    copies = []
    for i in range(sems.shape[0]):
        part = pl.ds(i * count, count)
        copies.append(pltpu.make_async_copy(f_ref.at[part], same_ref.at[part], sems.at[i]))
        copies[-1].start()
    rim_ref[...] = jnp.zeros_like(rim_ref)
    for i, copy in enumerate(copies):
        copy.wait()
        for v in range(i * count, (i + 1) * count):
            pack_rim(v, same_ref[v], rim_ref)


def iota(shape, dim):
    return lax.broadcasted_iota(jnp.int32, shape, dim)


def low_bits(x, size):
    return lax.rem(x, jnp.int32(size))


def weight_kernel(kin_ref, speed_ref, w_ref, dz_ref, shift_ref, scale_ref):
    nvars = kin_ref.shape[0]
    rows, columns = w_ref.shape[0] // 2, w_ref.shape[1]
    ny = rows // nvars
    spread = (iota((rows, nvars), 0) // ny == iota((rows, nvars), 1)).astype(F32)
    gather = (iota((nvars, columns), 1) // (2 * ny) == iota((nvars, columns), 0)).astype(F32)
    rates = exact(exact(spread, kin_ref[...]), gather)
    speed = exact(spread, speed_ref[...], ((1,), (1,)))[:, 1:2]
    row, column = iota((rows, columns), 0), iota((rows, columns), 1)
    y, other = low_bits(row, ny), low_bits(column, 2 * ny)
    iy = lax.axis_index("gy")
    below, above = iy > 0, iy < lax.axis_size("gy") - 1
    far = 8 * ny
    up = jnp.where(above, other - y, far)
    down = jnp.where(below, other - 2 * ny - y, far)
    offset = jnp.where(other < ny, other - y, jnp.where(other < ny + REACH, up, down))
    shifts = jnp.zeros((rows, columns), F32)
    for k in range(1, REACH + 1):
        shifts = jnp.where(offset == k, COEFFS[k - 1], jnp.where(offset == -k, -COEFFS[k - 1], shifts))
    shifts = jnp.where(row // ny == column // (2 * ny), speed * shifts, 0.0)
    high, low = split(TIME_STEP * (jnp.where(other == y, rates, 0.0) - shifts))
    w_ref[0:rows] = high
    w_ref[rows:] = low

    depth = dz_ref.shape[1]
    source, target = iota((depth, depth), 0), iota((depth, depth), 1)
    offset = source - target
    inner = jnp.zeros((depth, depth), F32)
    for k in range(1, REACH + 1):
        inner = jnp.where(offset == k, WHOLE[k - 1], jnp.where(offset == -k, -WHOLE[k - 1], inner))
    dz_ref[0:depth] = inner.astype(BF16)
    dz_ref[depth:] = inner.astype(BF16)
    turn = low_bits(target, REACH) - low_bits(source, REACH)
    first = source < depth // 2
    offset = REACH + jnp.where(first, turn, -turn)
    outer = jnp.zeros((depth, depth), F32)
    for k in range(1, REACH + 1):
        outer = jnp.where(offset == k, WHOLE[k - 1], outer)
    outer = jnp.where(source // REACH == target // REACH, jnp.where(first, -outer, outer), 0.0)
    shift_ref[...] = outer.astype(BF16)

    tile = scale_ref.shape[2:]
    for v in range(nvars):
        scale_ref[v, 0] = jnp.broadcast_to(TIME_STEP * speed_ref[0:1, v : v + 1], tile)
        scale_ref[v, 1] = jnp.broadcast_to(TIME_STEP / SCALE * speed_ref[2:3, v : v + 1], tile)


def project_kernel(zf_ref, zf_out_ref, wide_ref):
    depth, rank = zf_ref.shape[1], zf_ref.shape[0]
    identity = (iota((depth, depth), 0) == iota((depth, depth), 1)).astype(F32)
    wide_ref[...] = jnp.zeros_like(wide_ref)
    wide_ref[:, 0:rank] = exact(identity, zf_ref[...], ((1,), (1,)))
    high, low = split(wide_ref[...])
    zf_out_ref[0:depth, 0 : 2 * HALF] = high
    zf_out_ref[0:depth, 2 * HALF :] = low
    high, low = split(pltpu.roll(wide_ref[...], HALF, 1))
    zf_out_ref[depth:, 0 : 2 * HALF] = high
    zf_out_ref[depth:, 2 * HALF :] = low


def mix_planes(q_ref, beside_ref, w_ref, rate_ref):
    nvars, nx, ny, nz = q_ref.shape
    rows = nvars * ny

    def step(i, carry):
        high, low = [], []
        for p in (2 * i, 2 * i + 1):
            cells = jnp.concatenate([q_ref[:, p], beside_ref[:, p]], axis=1)
            h, l = split(cells.reshape(2 * rows, nz))
            high.append(h)
            low.append(l)
        both = dot(w_ref[...], jnp.concatenate(high, axis=1))
        total = both[:rows] + both[rows:] + dot(w_ref[0:rows], jnp.concatenate(low, axis=1))
        for j in range(2):
            rate_ref[:, 2 * i + j] = total[:, j * nz : (j + 1) * nz].reshape(nvars, ny, nz)
        return carry

    lax.fori_loop(0, nx // 2, step, 0, unroll=True)


def join_rims(first_ref, second_ref, shift_ref, rim_ref):
    nx, ny, nz = rim_ref.shape
    upper = lax.shift_right_logical(iota(rim_ref.shape, 2) * 2 // nz, 0)
    rim = jnp.where(upper == odd("gz"), second_ref[...], first_ref[...]).reshape(nx * ny, nz)
    high, low = split(rim)
    rim_ref[...] = (dot(high, shift_ref[...]) + dot(low, shift_ref[...])).reshape(rim_ref.shape)


def step_of(v, q_ref, first_ref, second_ref, dz_ref, rate_ref, rim_ref, scale_ref):
    _, nx, ny, nz = q_ref.shape
    q = q_ref[v]
    even = jnp.full((REACH, ny, nz), odd("gx")) == 0
    low_rim = jnp.where(even, second_ref[v], first_ref[v])
    high_rim = jnp.where(even, first_ref[v], second_ref[v])
    tall = jnp.concatenate([low_rim, q, high_rim], axis=0)
    gx = None
    for k in range(1, REACH + 1):
        part = COEFFS[k - 1] * (tall[REACH + k : REACH + k + nx] - tall[REACH - k : REACH - k + nx])
        gx = part if gx is None else gx + part
    high, low = split(q.reshape(nx * ny, nz))
    gz = dot(jnp.concatenate([high, low], axis=1), dz_ref[...]).reshape(nx, ny, nz)
    lane = lax.broadcasted_iota(jnp.int32, q.shape, 2)
    rim = rim_ref[...]
    first = pltpu.roll(rim, lax.rem(nz - REACH * v, nz), 2)
    last = pltpu.roll(rim, nz // 2 - REACH - REACH * v, 2)
    gz = gz + jnp.where(lane < REACH, first, jnp.where(lane >= nz - REACH, last, 0.0))
    return rate_ref[v] - scale_ref[v, 0] * gx - scale_ref[v, 1] * gz


def section_kernel(
    f_ref, x1_ref, x2_ref, beside_ref, z1_ref, z2_ref, w_ref, dz_ref, shift_ref, scale_ref,
    s_ref, first_ref, second_ref, out_rim_ref, rate_ref, rim_ref,
):
    mix_planes(f_ref, beside_ref, w_ref, rate_ref)
    join_rims(z1_ref, z2_ref, shift_ref, rim_ref)
    out_rim_ref[...] = jnp.zeros_like(out_rim_ref)

    def step(v, carry):
        s = f_ref[v] + step_of(v, f_ref, x1_ref, x2_ref, dz_ref, rate_ref, rim_ref, scale_ref)
        s_ref[v] = s
        low, high = s[:REACH], s[s.shape[0] - REACH :]
        even = jnp.full(low.shape, odd("gx")) == 0
        first_ref[v] = jnp.where(even, high, low)
        second_ref[v] = jnp.where(even, low, high)
        pack_rim(v, s, out_rim_ref)
        return carry

    lax.fori_loop(0, f_ref.shape[0], step, 0, unroll=4)


def next_kernel(
    f_ref, s_ref, x1_ref, x2_ref, beside_ref, z1_ref, z2_ref, w_ref, dz_ref, shift_ref, scale_ref, zf_ref,
    next_ref, *refs,
):
    _, nx, ny, nz = f_ref.shape
    chunk_refs, (rate_ref, rim_ref) = refs[:-2], refs[-2:]
    mix_planes(s_ref, beside_ref, w_ref, rate_ref)
    join_rims(z1_ref, z2_ref, shift_ref, rim_ref)
    count, pairs = len(chunk_refs), chunk_refs[0].shape[0]
    for k, chunk_ref in enumerate(chunk_refs):
        start = lax.rem(lax.axis_index("gz") + k, jnp.int32(count)) * (2 * pairs)
        for j in range(pairs):
            both = []
            for v in (start + 2 * j, start + 2 * j + 1):
                rate = step_of(v, s_ref, x1_ref, x2_ref, dz_ref, rate_ref, rim_ref, scale_ref)
                new = 0.5 * (f_ref[v] + s_ref[v] + rate)
                next_ref[v] = new
                both.append(new.reshape(nx * ny, nz))
            high, low = split(jnp.concatenate(both, axis=1))
            wide = dot(high, zf_ref[...])
            chunk_ref[j] = wide[:, : 2 * HALF] + wide[:, 2 * HALF :] + dot(low, zf_ref[:, : 2 * HALF])


def sum_kernel(*refs):
    total = refs[0][...]
    for ref in refs[1:-1]:
        total = total + ref[...]
    refs[-1][...] = total


def store_kernel(in_ref, out_ref, sem):
    copy = pltpu.make_async_copy(in_ref, out_ref, sem)
    copy.start()
    copy.wait()


def factor_kernel(xf_ref, *refs):
    y_refs, (out_ref, xt_ref) = refs[:-2], refs[-2:]
    planes, a_count = xf_ref.shape[0], xt_ref.shape[0]
    ny = y_refs[0].shape[0]
    width = planes * ny
    b_count = out_ref.shape[1] // a_count

    def own(count, total, place):
        return (iota((count, total), 1) == iota((count, total), 0) + place * count).astype(F32)

    mine = exact(own(a_count, xf_ref.shape[1], lax.axis_index("gx")), xf_ref[...], ((1,), (1,)))
    spread = iota((planes, width), 0) == iota((planes, width), 1) // ny
    xt_ref[...] = exact(mine, spread.astype(F32))
    spread = iota((ny, width), 0) == low_bits(iota((ny, width), 1), ny)
    for i, y_ref in enumerate(y_refs):
        rows = exact(own(b_count, y_ref.shape[1], lax.axis_index("gy")), y_ref[...], ((1,), (1,)))
        yt = exact(rows, spread.astype(F32))
        for a in range(a_count):
            high, low = split(xt_ref[a : a + 1, :] * yt)
            out_ref[0, a * b_count : (a + 1) * b_count, i * width : (i + 1) * width] = high
            out_ref[1, a * b_count : (a + 1) * b_count, i * width : (i + 1) * width] = low


def core_kernel(rank_ref, q_ref, *refs):
    block_refs, (out_ref, placed_ref, result_ref, sems) = refs[:-4], refs[-4:]
    pairs, blocks_y, planes, ny, nz = placed_ref.shape
    nx = block_refs[0].shape[1] // ny
    rank = out_ref.shape[2]
    rows = out_ref.shape[1] // sems.shape[0]
    for i in range(planes // nx):
        for x in range(nx):
            row = rank_ref[i * nx + x]
            for j in range(blocks_y):
                for p in range(pairs):
                    block_ref = block_refs[i * blocks_y + j]
                    placed_ref[p, j, row] = block_ref[p, x * ny : (x + 1) * ny, :]
    columns = [placed_ref[p].reshape(blocks_y * planes * ny, nz) for p in range(pairs)]
    high, low = split(jnp.concatenate(columns, axis=1))
    copies = []
    for m in range(sems.shape[0]):
        here = slice(m * rows, (m + 1) * rows)
        q_high = q_ref[0, here]
        result = dot(q_high, high) + (dot(q_high, low) + dot(q_ref[1, here], high))
        for v in range(2 * pairs):
            result_ref[v, here] = result[:, v * HALF : v * HALF + rank]
        copies.append(pltpu.make_async_copy(result_ref.at[:, here], out_ref.at[:, here], sems.at[m]))
        copies[-1].start()
    for copy in copies:
        copy.wait()


def shifted(x, axis, k):
    count = lax.axis_size(axis)
    return lax.ppermute(x, axis, [(i, (i + k) % count) for i in range(count)])


def gathered(x, axis):
    count = lax.axis_size(axis)
    if count <= 4:
        return [x] + [shifted(x, axis, k) for k in range(1, count)]
    blocks = lax.all_gather(x, axis)
    return [blocks[k] for k in range(count)]


def gathered_on_chip(x):
    count = lax.axis_size("gx")
    if count != 4 or lax.axis_size("gy") != 2:
        return gathered(x, "gx")
    ring = [((i, j), ((i + (1, 3)[j]) % 4, j)) for i in range(4) for j in range(2)]
    mine = lax.ppermute(x, ("gx", "gy"), [(2 * i + j, 2 * k + l) for (i, j), (k, l) in ring])
    across = shifted(x, "gx", 2)
    theirs = lax.ppermute(mine, "gy", [(0, 1), (1, 0)])
    upper = lax.axis_index("gy") == 1
    return [x, jnp.where(upper, theirs, mine), across, jnp.where(upper, mine, theirs)]


def paired(first, second, axis):
    out = []
    for x, start in ((first, 0), (second, 1)):
        links = [(i, i + 1) for i in range(start, lax.axis_size(axis) - 1, 2)]
        out.append(lax.ppermute(x, axis, links + [(j, i) for i, j in links]))
    return out


def beside(block, axis):
    count = lax.axis_size(axis)
    if count == 2:
        return lax.ppermute(block, axis, [(0, 1), (1, 0)])
    from_low = lax.ppermute(block, axis, [(i, i + 1) for i in range(count - 1)])
    from_high = lax.ppermute(block, axis, [(i + 1, i) for i in range(count - 1)])
    row = lax.broadcasted_iota(jnp.int32, block.shape, 2)
    return jnp.where(row < REACH, from_high, from_low)


def local(fields, speeds, kinetics, block_rank, x_factor, y_factor, z_factor):
    nvars, nx, ny, nz = fields.shape
    rank = z_factor.shape[1]
    gx, gy, gz = (lax.axis_size(axis) for axis in ("gx", "gy", "gz"))
    rim = (nvars, REACH, ny, nz)
    plane = (nx, ny, nz)
    scratch = [pltpu.VMEM(fields.shape, F32), pltpu.VMEM(plane, F32)]
    pairs = nvars // 2 // gz
    chunk = (pairs, nx * ny, 2 * HALF)
    barrier = lax.optimization_barrier

    first, second = call(
        rim_kernel,
        [(rim, F32), (rim, F32)],
        [HBM],
        (fields,),
        [pltpu.SemaphoreType.DMA((2,))],
    )
    x1, x2 = paired(first, second, "gx")
    packed, same = call(
        pack_kernel, [(plane, F32), (fields.shape, F32)], [HBM], (fields,), [pltpu.SemaphoreType.DMA((4,))]
    )
    z1, z2 = paired(packed, packed, "gz")
    other = beside(fields, "gy")
    weights, dz, rim_shift, scales = call(
        weight_kernel,
        [((2 * nvars * ny, 2 * nvars * ny), BF16), ((2 * nz, nz), BF16), ((nz, nz), BF16), ((nvars, 2, ny, nz), F32)],
        [VMEM] * 2,
        (kinetics, speeds),
    )
    section, first, second, packed = call(
        section_kernel,
        [(fields.shape, F32), (rim, F32), (rim, F32), (plane, F32)],
        [VMEM] * 10,
        (same, x1, x2, other, z1, z2, weights, dz, rim_shift, scales),
        scratch,
    )
    a_count, b_count = x_factor.shape[1] // gx, y_factor.shape[1] // gy
    rows, planes = a_count * b_count, gx * nx
    cells = planes * gy * ny
    section, first, second, packed, z_factor, x_factor, y_factor = barrier(
        (section, first, second, packed, z_factor, x_factor, y_factor)
    )
    x1, x2 = paired(first, second, "gx")
    z1, z2 = paired(packed, packed, "gz")
    other = beside(section, "gy")
    y_rows = gathered(y_factor, "gy")
    (zf,) = call(project_kernel, [((2 * nz, 4 * HALF), BF16)], [VMEM], (z_factor.T,), [pltpu.VMEM((nz, 2 * HALF), F32)])
    (factor,) = call(
        factor_kernel,
        [((2, rows, cells), BF16)],
        [VMEM] * (1 + gy),
        (x_factor, *y_rows),
        [pltpu.VMEM((a_count, planes * ny), F32)],
    )
    x1, x2, z1, z2, other, zf, factor = barrier((x1, x2, z1, z2, other, zf, factor))
    new, *chunks = call(
        next_kernel,
        [(fields.shape, F32)] + [(chunk, F32)] * gz,
        [VMEM] * 12,
        (same, section, x1, x2, other, z1, z2, weights, dz, rim_shift, scales, zf),
        scratch,
    )
    new, chunks, block_rank = barrier((new, chunks, block_rank))
    parts = [chunks[0]] + [shifted(chunks[k], "gz", k) for k in range(1, gz)]
    ranks = jnp.concatenate(gathered_on_chip(block_rank), axis=0)
    (fields_next,) = call(store_kernel, [(fields.shape, F32)], [ANY], (new,), [pltpu.SemaphoreType.DMA], out_spec=HBM)
    (own,) = call(sum_kernel, [(chunk, F32)], [VMEM] * gz, parts)
    blocks = [gathered(block, "gy") for block in gathered(own, "gx")]
    pieces = 4 if rows % 128 == 0 else 1
    (core,) = call(
        core_kernel,
        [((2 * pairs, rows, rank), F32)],
        [SMEM] + [VMEM] * (1 + gx * gy),
        (ranks, factor, *(block for line in blocks for block in line)),
        [
            pltpu.VMEM((pairs, gy, planes, ny, nz), F32),
            pltpu.VMEM((2 * pairs, rows, rank), F32),
            pltpu.SemaphoreType.DMA((pieces,)),
        ],
        room=16 if cells <= 1024 else 56,
        out_spec=HBM,
    )
    return fields_next, core.reshape(2 * pairs, a_count, b_count, rank)


def solution(mesh):
    placed = (P(None, "gx", "gy", "gz"), P(), P(), P("gx"), P(), P("gy", None), P("gz", None))
    return jax.shard_map(
        local,
        mesh=mesh,
        in_specs=placed,
        out_specs=(P(None, "gx", "gy", "gz"), P("gz", "gx", "gy", None)),
        check_vma=False,
    )
```

```python
import jax
import jax.numpy as jnp
from jax import lax
from jax.experimental import pallas as pl
from jax.experimental.pallas import tpu as pltpu
from jax.sharding import PartitionSpec as P

COEFFS = (0.8, -0.2, 4.0 / 105.0, -1.0 / 280.0)
SCALE = 840.0
WHOLE = (672.0, -168.0, 32.0, -3.0)
TIME_STEP = 0.45
REACH = len(COEFFS)
HALF = 64
F32, BF16 = jnp.float32, jnp.bfloat16
HIGHEST = lax.Precision.HIGHEST
VMEM = pl.BlockSpec(memory_space=pltpu.VMEM)
SMEM = pl.BlockSpec(memory_space=pltpu.SMEM)
ANY = pl.BlockSpec(memory_space=pl.ANY)
HBM = pl.BlockSpec(memory_space=pltpu.HBM)


def call(kernel, out_shapes, in_specs, args, scratch=(), room=16, out_spec=VMEM):
    return pl.pallas_call(
        kernel,
        out_shape=tuple(jax.ShapeDtypeStruct(s, d) for s, d in out_shapes),
        in_specs=in_specs,
        out_specs=tuple(out_spec for _ in out_shapes),
        scratch_shapes=list(scratch),
        compiler_params=pltpu.CompilerParams(vmem_limit_bytes=room * 2**20),
    )(*args)


def dot(a, b):
    return jnp.dot(a, b, preferred_element_type=F32)


def exact(a, b, dims=((1,), (0,))):
    return lax.dot_general(a, b, (dims, ((), ())), precision=HIGHEST, preferred_element_type=F32)


def split(x):
    high = x.astype(BF16)
    return high, (x - high.astype(F32)).astype(BF16)


def odd(axis):
    return lax.rem(lax.axis_index(axis), jnp.int32(2))


def rim_kernel(f_ref, first_ref, second_ref, sems):
    top, parity = f_ref.shape[1] - REACH, odd("gx")
    copies = [
        pltpu.make_async_copy(f_ref.at[:, pl.ds(start, REACH)], target, sems.at[i])
        for i, (start, target) in enumerate(((top * (1 - parity), first_ref), (top * parity, second_ref)))
    ]
    for copy in copies:
        copy.start()
    for copy in copies:
        copy.wait()


def pack_rim(v, values, rim_ref):
    width = values.shape[2]
    group = lax.shift_right_logical(lax.broadcasted_iota(jnp.int32, values.shape, 2), 2)
    last = pltpu.roll(values, REACH * v + REACH, 2)
    first = pltpu.roll(values, width // 2 + REACH * v, 2)
    rim = jnp.where(group == v, last, rim_ref[...])
    rim_ref[...] = jnp.where(group == v + width // 2 // REACH, first, rim)


def pack_kernel(f_ref, zf_ref, rim_ref, same_ref, pad_ref, sems):
    count = f_ref.shape[0] // sems.shape[0]
    copies = []
    for i in range(sems.shape[0]):
        part = pl.ds(i * count, count)
        copies.append(pltpu.make_async_copy(f_ref.at[part], same_ref.at[part], sems.at[i]))
        copies[-1].start()
    rim_ref[...] = jnp.zeros_like(rim_ref)
    nx = rim_ref.shape[0] - 1
    depth = zf_ref.shape[1]
    row = iota((2 * REACH, depth), 0)
    wanted = jnp.where(row < REACH, row + depth - REACH, row - REACH)
    pick = (iota((2 * REACH, depth), 1) == wanted).astype(F32)
    pad_ref[...] = jnp.zeros_like(pad_ref)
    pad_ref[:, 0 : zf_ref.shape[0]] = exact(pick, zf_ref[...], ((1,), (1,)))
    rim_ref[nx] = pad_ref[...]
    planes_ref = rim_ref.at[pl.ds(0, nx)]
    for i, copy in enumerate(copies):
        copy.wait()
        for v in range(i * count, (i + 1) * count):
            pack_rim(v, same_ref[v], planes_ref)


def iota(shape, dim):
    return lax.broadcasted_iota(jnp.int32, shape, dim)


def low_bits(x, size):
    return lax.rem(x, jnp.int32(size))


def weight_kernel(kin_ref, speed_ref, w_ref, dz_ref, shift_ref, scale_ref, pair_ref):
    nvars = kin_ref.shape[0]
    rows, columns = w_ref.shape[0] // 2, w_ref.shape[1]
    ny = rows // nvars
    spread = (iota((rows, nvars), 0) // ny == iota((rows, nvars), 1)).astype(F32)
    gather = (iota((nvars, columns), 1) // (2 * ny) == iota((nvars, columns), 0)).astype(F32)
    rates = exact(exact(spread, kin_ref[...]), gather)
    speed = exact(spread, speed_ref[...], ((1,), (1,)))[:, 1:2]
    row, column = iota((rows, columns), 0), iota((rows, columns), 1)
    y, other = low_bits(row, ny), low_bits(column, 2 * ny)
    iy = lax.axis_index("gy")
    below, above = iy > 0, iy < lax.axis_size("gy") - 1
    far = 8 * ny
    up = jnp.where(above, other - y, far)
    down = jnp.where(below, other - 2 * ny - y, far)
    offset = jnp.where(other < ny, other - y, jnp.where(other < ny + REACH, up, down))
    shifts = jnp.zeros((rows, columns), F32)
    for k in range(1, REACH + 1):
        shifts = jnp.where(offset == k, COEFFS[k - 1], jnp.where(offset == -k, -COEFFS[k - 1], shifts))
    shifts = jnp.where(row // ny == column // (2 * ny), speed * shifts, 0.0)
    high, low = split(TIME_STEP * (jnp.where(other == y, rates, 0.0) - shifts))
    w_ref[0:rows] = high
    w_ref[rows:] = low

    depth = dz_ref.shape[1]
    source, target = iota((depth, depth), 0), iota((depth, depth), 1)
    offset = source - target
    inner = jnp.zeros((depth, depth), F32)
    for k in range(1, REACH + 1):
        inner = jnp.where(offset == k, WHOLE[k - 1], jnp.where(offset == -k, -WHOLE[k - 1], inner))
    dz_ref[0:depth] = inner.astype(BF16)
    dz_ref[depth:] = inner.astype(BF16)
    turn = low_bits(target, REACH) - low_bits(source, REACH)
    first = source < depth // 2
    offset = REACH + jnp.where(first, turn, -turn)
    outer = jnp.zeros((depth, depth), F32)
    for k in range(1, REACH + 1):
        outer = jnp.where(offset == k, WHOLE[k - 1], outer)
    outer = jnp.where(source // REACH == target // REACH, jnp.where(first, -outer, outer), 0.0)
    shift_ref[...] = outer.astype(BF16)

    tile = scale_ref.shape[2:]
    for v in range(nvars):
        scale_ref[v, 0] = jnp.broadcast_to(TIME_STEP * speed_ref[0:1, v : v + 1], tile)
        scale_ref[v, 1] = jnp.broadcast_to(TIME_STEP / SCALE * speed_ref[2:3, v : v + 1], tile)
    even = iota(tile, 1) < HALF
    for p in range(nvars // 2):
        for i in range(2):
            pair_ref[p, i] = 0.5 * jnp.where(even, scale_ref[2 * p, i], scale_ref[2 * p + 1, i])


def lay_out(wide_ref, out_ref):
    depth = wide_ref.shape[0]
    for start, table in ((0, wide_ref[...]), (depth, pltpu.roll(wide_ref[...], HALF, 1))):
        high, low = split(table)
        out_ref[start : start + depth, 0 : 2 * HALF] = high
        out_ref[start : start + depth, 2 * HALF :] = low


def project_kernel(zf_ref, out_ref, wide_ref):
    depth, rank = zf_ref.shape[1], zf_ref.shape[0]
    identity = (iota((depth, depth), 0) == iota((depth, depth), 1)).astype(F32)
    wide_ref[...] = jnp.zeros_like(wide_ref)
    wide_ref[:, 0:rank] = exact(identity, zf_ref[...], ((1,), (1,)))
    lay_out(wide_ref, out_ref)


def adjoint_kernel(zf_ref, z1_ref, z2_ref, dz_ref, out_ref, wide_ref):
    depth, rank = zf_ref.shape[1], zf_ref.shape[0]
    last = z1_ref.shape[0] - 1
    wide_ref[...] = jnp.zeros_like(wide_ref)
    wide_ref[:, 0:rank] = exact(dz_ref[0:depth].astype(F32), zf_ref[...], ((1,), (1,)))
    upper = iota(z1_ref.shape[1:], 0) // REACH
    rows = jnp.where(upper == odd("gz"), z2_ref[last], z1_ref[last])
    source, place = iota((depth, 2 * REACH), 0), iota((depth, 2 * REACH), 1)
    below = place < REACH
    offset = jnp.where(below, source + REACH - place, depth + place - REACH - source)
    reach = jnp.zeros((depth, 2 * REACH), F32)
    for k in range(1, REACH + 1):
        reach = jnp.where(offset == k, WHOLE[k - 1], reach)
    wide_ref[...] = wide_ref[...] + exact(jnp.where(below, reach, -reach), rows)
    lay_out(wide_ref, out_ref)


def projected(pair, zf_ref):
    high, low = split(pair)
    wide = dot(high, zf_ref[...])
    return wide[:, : 2 * HALF] + wide[:, 2 * HALF :] + dot(low, zf_ref[:, : 2 * HALF])


def mix_planes(q_ref, beside_ref, w_ref, rate_ref):
    nvars, nx, ny, nz = q_ref.shape
    rows = nvars * ny

    def step(i, carry):
        high, low = [], []
        for p in (2 * i, 2 * i + 1):
            cells = jnp.concatenate([q_ref[:, p], beside_ref[:, p]], axis=1)
            h, l = split(cells.reshape(2 * rows, nz))
            high.append(h)
            low.append(l)
        both = dot(w_ref[...], jnp.concatenate(high, axis=1))
        total = both[:rows] + both[rows:] + dot(w_ref[0:rows], jnp.concatenate(low, axis=1))
        for j in range(2):
            rate_ref[:, 2 * i + j] = total[:, j * nz : (j + 1) * nz].reshape(nvars, ny, nz)
        return carry

    lax.fori_loop(0, nx // 2, step, 0, unroll=True)


def join_rims(first_ref, second_ref, shift_ref, rim_ref):
    nx, ny, nz = rim_ref.shape
    upper = lax.shift_right_logical(iota(rim_ref.shape, 2) * 2 // nz, 0)
    rim = jnp.where(upper == odd("gz"), second_ref[0:nx], first_ref[0:nx]).reshape(nx * ny, nz)
    high, low = split(rim)
    rim_ref[...] = (dot(high, shift_ref[...]) + dot(low, shift_ref[...])).reshape(rim_ref.shape)


def z_slope(v, q, dz_ref, rim_ref):
    nx, ny, nz = q.shape
    high, low = split(q.reshape(nx * ny, nz))
    slope = dot(jnp.concatenate([high, low], axis=1), dz_ref[...]).reshape(nx, ny, nz)
    lane = lax.broadcasted_iota(jnp.int32, q.shape, 2)
    rim = rim_ref[...]
    first = pltpu.roll(rim, lax.rem(nz - REACH * v, nz), 2)
    last = pltpu.roll(rim, nz // 2 - REACH - REACH * v, 2)
    return slope + jnp.where(lane < REACH, first, jnp.where(lane >= nz - REACH, last, 0.0))


def x_slope(low_rim, q, high_rim):
    nx = q.shape[0]
    tall = jnp.concatenate([low_rim, q, high_rim], axis=0)
    slope = None
    for k in range(1, REACH + 1):
        part = COEFFS[k - 1] * (tall[REACH + k : REACH + k + nx] - tall[REACH - k : REACH - k + nx])
        slope = part if slope is None else slope + part
    return slope


def rim_slopes(low_rim, high_rim):
    first, last = [], []
    for p in range(REACH):
        under = over = None
        for k in range(p + 1, REACH + 1):
            term = COEFFS[k - 1] * low_rim[REACH + p - k]
            under = term if under is None else under + term
        for k in range(REACH - p, REACH + 1):
            term = COEFFS[k - 1] * high_rim[p + k - REACH]
            over = term if over is None else over + term
        first.append(-under[None])
        last.append(over[None])
    return jnp.concatenate(first, axis=0), jnp.concatenate(last, axis=0)


def by_side(first, second):
    even = jnp.full(first.shape, odd("gx")) == 0
    return jnp.where(even, second, first), jnp.where(even, first, second)


def section_kernel(
    f_ref, x1_ref, x2_ref, beside_ref, z1_ref, z2_ref, w_ref, dz_ref, shift_ref, scale_ref, zf_ref,
    s_ref, first_ref, second_ref, out_rim_ref, u1_ref, u2_ref, rate_ref, rim_ref,
):
    nvars, nx, ny, nz = f_ref.shape
    mix_planes(f_ref, beside_ref, w_ref, rate_ref)
    join_rims(z1_ref, z2_ref, shift_ref, rim_ref)
    out_rim_ref[...] = jnp.zeros_like(out_rim_ref)

    def step(p, carry):
        both = []
        for v in (2 * p, 2 * p + 1):
            f = f_ref[v]
            low_rim, high_rim = by_side(x1_ref[v], x2_ref[v])
            slope = scale_ref[v, 0] * x_slope(low_rim, f, high_rim)
            s = f + rate_ref[v] - slope - scale_ref[v, 1] * z_slope(v, f, dz_ref, rim_ref)
            s_ref[v] = s
            second, first = by_side(s[nx - REACH :], s[:REACH])
            first_ref[v] = first
            second_ref[v] = second
            pack_rim(v, s, out_rim_ref)
            both.append(jnp.concatenate([first, second], axis=0).reshape(2 * REACH * ny, nz))
        u = projected(jnp.concatenate(both, axis=1), zf_ref)
        u1_ref[p] = u[: REACH * ny].reshape(REACH, ny, 2 * HALF)
        u2_ref[p] = u[REACH * ny :].reshape(REACH, ny, 2 * HALF)
        return carry

    lax.fori_loop(0, nvars // 2, step, 0, unroll=2)


def chunk_pairs(chunk_refs):
    count, pairs = len(chunk_refs), chunk_refs[0].shape[0]
    for k in range(count):
        start = lax.rem(lax.axis_index("gz") + k, jnp.int32(count)) * pairs
        for j in range(pairs):
            yield k, j, start + j


def near_kernel(
    f_ref, s_ref, beside_ref, w_ref, scale_ref, pair_ref, zf_ref, adjoint_ref,
    hold_ref, *refs,
):
    _, nx, ny, nz = f_ref.shape
    chunk_refs, rate_ref = refs[:-1], refs[-1]
    mix_planes(s_ref, beside_ref, w_ref, rate_ref)
    nothing = jnp.zeros((REACH, ny, nz), F32)
    for k, j, p in chunk_pairs(chunk_refs):
        holds, sections = [], []
        for v in (2 * p, 2 * p + 1):
            s = s_ref[v]
            rate = rate_ref[v] - scale_ref[v, 0] * x_slope(nothing, s, nothing)
            hold = 0.5 * (f_ref[v] + s + rate)
            hold_ref[v] = hold
            holds.append(hold.reshape(nx * ny, nz))
            sections.append(s.reshape(nx * ny, nz))
        slope = projected(jnp.concatenate(sections, axis=1), adjoint_ref).reshape(nx, ny, 2 * HALF)
        total = projected(jnp.concatenate(holds, axis=1), zf_ref).reshape(nx, ny, 2 * HALF)
        chunk_refs[k][j] = (total - pair_ref[p, 1] * slope).reshape(nx * ny, 2 * HALF)


def far_kernel(u1_ref, u2_ref, pair_ref, *refs):
    count = len(refs) // 2
    edge = REACH * u1_ref.shape[2]
    rows = refs[0].shape[1]
    for k, j, p in chunk_pairs(refs[count:]):
        old_ref, new_ref = refs[k], refs[count + k]
        low_rim, high_rim = by_side(u1_ref[p], u2_ref[p])
        first, last = rim_slopes(low_rim, high_rim)
        scale = pair_ref[p, 0]
        new_ref[j, :edge] = old_ref[j, :edge] - (scale * first).reshape(edge, 2 * HALF)
        new_ref[j, edge : rows - edge] = old_ref[j, edge : rows - edge]
        new_ref[j, rows - edge :] = old_ref[j, rows - edge :] - (scale * last).reshape(edge, 2 * HALF)


def finish_kernel(
    hold_ref, s_ref, x1_ref, x2_ref, z1_ref, z2_ref, dz_ref, shift_ref, scale_ref, out_ref, next_ref, rim_ref, sems
):
    nvars, nx, _, _ = hold_ref.shape
    join_rims(z1_ref, z2_ref, shift_ref, rim_ref)
    count = nvars // sems.shape[0]
    copies = []
    for i in range(sems.shape[0]):
        for v in range(i * count, (i + 1) * count):
            slope = scale_ref[v, 1] * z_slope(v, s_ref[v], dz_ref, rim_ref)
            first, last = rim_slopes(*by_side(x1_ref[v], x2_ref[v]))
            next_ref[v] = hold_ref[v] - 0.5 * slope
            next_ref[v, :REACH] -= 0.5 * scale_ref[v, 0] * first
            next_ref[v, nx - REACH :] -= 0.5 * scale_ref[v, 0] * last
        part = pl.ds(i * count, count)
        copies.append(pltpu.make_async_copy(next_ref.at[part], out_ref.at[part], sems.at[i]))
        copies[-1].start()
    for copy in copies:
        copy.wait()


def sum_kernel(*refs):
    total = refs[0][...]
    for ref in refs[1:-1]:
        total = total + ref[...]
    refs[-1][...] = total


def factor_kernel(xf_ref, *refs):
    y_refs, (out_ref, xt_ref) = refs[:-2], refs[-2:]
    planes, a_count = xf_ref.shape[0], xt_ref.shape[0]
    ny = y_refs[0].shape[0]
    width = planes * ny
    b_count = out_ref.shape[1] // a_count

    def own(count, total, place):
        return (iota((count, total), 1) == iota((count, total), 0) + place * count).astype(F32)

    mine = exact(own(a_count, xf_ref.shape[1], lax.axis_index("gx")), xf_ref[...], ((1,), (1,)))
    spread = iota((planes, width), 0) == iota((planes, width), 1) // ny
    xt_ref[...] = exact(mine, spread.astype(F32))
    spread = iota((ny, width), 0) == low_bits(iota((ny, width), 1), ny)
    for i, y_ref in enumerate(y_refs):
        rows = exact(own(b_count, y_ref.shape[1], lax.axis_index("gy")), y_ref[...], ((1,), (1,)))
        yt = exact(rows, spread.astype(F32))
        for a in range(a_count):
            high, low = split(xt_ref[a : a + 1, :] * yt)
            out_ref[0, a * b_count : (a + 1) * b_count, i * width : (i + 1) * width] = high
            out_ref[1, a * b_count : (a + 1) * b_count, i * width : (i + 1) * width] = low


def core_kernel(rank_ref, q_ref, *refs):
    block_refs, (out_ref, placed_ref, result_ref, sems) = refs[:-4], refs[-4:]
    pairs, blocks_y, planes, ny, nz = placed_ref.shape
    nx = block_refs[0].shape[1] // ny
    rank = out_ref.shape[2]
    rows = out_ref.shape[1] // sems.shape[0]
    for i in range(planes // nx):
        for x in range(nx):
            row = rank_ref[i * nx + x]
            for j in range(blocks_y):
                for p in range(pairs):
                    block_ref = block_refs[i * blocks_y + j]
                    placed_ref[p, j, row] = block_ref[p, x * ny : (x + 1) * ny, :]
    columns = [placed_ref[p].reshape(blocks_y * planes * ny, nz) for p in range(pairs)]
    high, low = split(jnp.concatenate(columns, axis=1))
    copies = []
    for m in range(sems.shape[0]):
        here = slice(m * rows, (m + 1) * rows)
        q_high = q_ref[0, here]
        result = dot(q_high, high) + (dot(q_high, low) + dot(q_ref[1, here], high))
        for v in range(2 * pairs):
            result_ref[v, here] = result[:, v * HALF : v * HALF + rank]
        copies.append(pltpu.make_async_copy(result_ref.at[:, here], out_ref.at[:, here], sems.at[m]))
        copies[-1].start()
    for copy in copies:
        copy.wait()


def shifted(x, axis, k):
    count = lax.axis_size(axis)
    return lax.ppermute(x, axis, [(i, (i + k) % count) for i in range(count)])


def gathered(x, axis):
    count = lax.axis_size(axis)
    if count <= 4:
        return [x] + [shifted(x, axis, k) for k in range(1, count)]
    blocks = lax.all_gather(x, axis)
    return [blocks[k] for k in range(count)]


def gathered_on_chip(x):
    count = lax.axis_size("gx")
    if count != 4 or lax.axis_size("gy") != 2:
        return gathered(x, "gx")
    ring = [((i, j), ((i + (1, 3)[j]) % 4, j)) for i in range(4) for j in range(2)]
    mine = lax.ppermute(x, ("gx", "gy"), [(2 * i + j, 2 * k + l) for (i, j), (k, l) in ring])
    across = shifted(x, "gx", 2)
    theirs = lax.ppermute(mine, "gy", [(0, 1), (1, 0)])
    upper = lax.axis_index("gy") == 1
    return [x, jnp.where(upper, theirs, mine), across, jnp.where(upper, mine, theirs)]


def paired_once(x, axis, start):
    links = [(i, i + 1) for i in range(start, lax.axis_size(axis) - 1, 2)]
    return (lax.ppermute(x, axis, links + [(j, i) for i, j in links]),)


def paired(first, second, axis):
    out = ()
    for x, start in ((first, 0), (second, 1)):
        out += paired_once(x, axis, start)
    return out


def beside(block, axis):
    count = lax.axis_size(axis)
    if count == 2:
        return lax.ppermute(block, axis, [(0, 1), (1, 0)])
    from_low = lax.ppermute(block, axis, [(i, i + 1) for i in range(count - 1)])
    from_high = lax.ppermute(block, axis, [(i + 1, i) for i in range(count - 1)])
    row = lax.broadcasted_iota(jnp.int32, block.shape, 2)
    return jnp.where(row < REACH, from_high, from_low)


def local(fields, speeds, kinetics, block_rank, x_factor, y_factor, z_factor):
    nvars, nx, ny, nz = fields.shape
    rank = z_factor.shape[1]
    gx, gy, gz = (lax.axis_size(axis) for axis in ("gx", "gy", "gz"))
    rim = (nvars, REACH, ny, nz)
    plane = (nx, ny, nz)
    u_rim = (nvars // 2, REACH, ny, 2 * HALF)
    table = ((2 * nz, 4 * HALF), BF16)
    wide = pltpu.VMEM((nz, 2 * HALF), F32)
    pairs = nvars // 2 // gz
    chunk = (pairs, nx * ny, 2 * HALF)
    a_count, b_count = x_factor.shape[1] // gx, y_factor.shape[1] // gy
    rows, planes = a_count * b_count, gx * nx
    cells = planes * gy * ny
    barrier = lax.optimization_barrier
    transposed = z_factor.T

    first, second = call(
        rim_kernel, [(rim, F32), (rim, F32)], [HBM], (fields,), [pltpu.SemaphoreType.DMA((2,))]
    )
    x1, x2 = paired(first, second, "gx")
    packed, same = call(
        pack_kernel,
        [((nx + 1, ny, nz), F32), (fields.shape, F32)],
        [HBM, VMEM],
        (fields, transposed),
        [pltpu.VMEM((2 * REACH, nz), F32), pltpu.SemaphoreType.DMA((4,))],
    )
    z1, z2 = paired(packed, packed, "gz")
    other = beside(fields, "gy")
    weights, dz, rim_shift, scales, pair_scales = call(
        weight_kernel,
        [
            ((2 * nvars * ny, 2 * nvars * ny), BF16),
            ((2 * nz, nz), BF16),
            ((nz, nz), BF16),
            ((nvars, 2, ny, nz), F32),
            ((nvars // 2, 2, ny, nz), F32),
        ],
        [VMEM] * 2,
        (kinetics, speeds),
    )
    (zf,) = call(project_kernel, [table], [VMEM], (transposed,), [wide])
    section, first, second, packed, u1, u2 = call(
        section_kernel,
        [(fields.shape, F32), (rim, F32), (rim, F32), (plane, F32), (u_rim, F32), (u_rim, F32)],
        [VMEM] * 11,
        (same, x1, x2, other, z1, z2, weights, dz, rim_shift, scales, zf),
        [pltpu.VMEM(fields.shape, F32), pltpu.VMEM(plane, F32)],
    )
    section, first, second, packed, u1, u2, transposed, x_factor, y_factor = barrier(
        (section, first, second, packed, u1, u2, transposed, x_factor, y_factor)
    )
    other = beside(section, "gy")
    u1, u2 = paired(u1, u2, "gx")
    (x1,) = paired_once(first, "gx", 0)
    (adjoint,) = call(adjoint_kernel, [table], [VMEM] * 4, (transposed, z1, z2, dz), [wide])
    hold, *chunks = call(
        near_kernel,
        [(fields.shape, F32)] + [(chunk, F32)] * gz,
        [VMEM] * 8,
        (same, section, other, weights, scales, pair_scales, zf, adjoint),
        [pltpu.VMEM(fields.shape, F32)],
    )
    chunks = call(
        far_kernel, [(chunk, F32)] * gz, [VMEM] * (3 + gz), (u1, u2, pair_scales, *chunks)
    )
    chunks, block_rank, second, packed, hold = barrier((chunks, block_rank, second, packed, hold))
    parts = [chunks[0]] + [shifted(chunks[k], "gz", k) for k in range(1, gz)]
    ranks = jnp.concatenate(gathered_on_chip(block_rank), axis=0)
    (x2,) = paired_once(second, "gx", 1)
    y_rows = gathered(y_factor, "gy")
    (factor,) = call(
        factor_kernel,
        [((2, rows, cells), BF16)],
        [VMEM] * (1 + gy),
        (x_factor, *y_rows),
        [pltpu.VMEM((a_count, planes * ny), F32)],
    )
    (own,) = call(sum_kernel, [(chunk, F32)], [VMEM] * gz, parts)
    blocks = [gathered(block, "gy") for block in gathered(own, "gx")]
    z1, z2 = paired(packed, packed, "gz")
    (fields_next,) = call(
        finish_kernel,
        [(fields.shape, F32)],
        [VMEM] * 9,
        (hold, section, x1, x2, z1, z2, dz, rim_shift, scales),
        [pltpu.VMEM(fields.shape, F32), pltpu.VMEM(plane, F32), pltpu.SemaphoreType.DMA((4,))],
        out_spec=HBM,
    )
    pieces = 4 if rows % 128 == 0 else 1
    (core,) = call(
        core_kernel,
        [((2 * pairs, rows, rank), F32)],
        [SMEM] + [VMEM] * (1 + gx * gy),
        (ranks, factor, *(block for line in blocks for block in line)),
        [
            pltpu.VMEM((pairs, gy, planes, ny, nz), F32),
            pltpu.VMEM((2 * pairs, rows, rank), F32),
            pltpu.SemaphoreType.DMA((pieces,)),
        ],
        room=16 if cells <= 1024 else 56,
        out_spec=HBM,
    )
    return fields_next, core.reshape(2 * pairs, a_count, b_count, rank)


def solution(mesh):
    placed = (P(None, "gx", "gy", "gz"), P(), P(), P("gx"), P(), P("gy", None), P("gz", None))
    return jax.shard_map(
        local,
        mesh=mesh,
        in_specs=placed,
        out_specs=(P(None, "gx", "gy", "gz"), P("gz", "gx", "gy", None)),
        check_vma=False,
    )
```

```python
import functools

import jax
import jax.numpy as jnp
from jax import lax
from jax.experimental import pallas as pl
from jax.experimental.pallas import tpu as pltpu
from jax.sharding import PartitionSpec as P

COEFFS = (0.8, -0.2, 4.0 / 105.0, -1.0 / 280.0)
SCALE = 840.0
WHOLE = (672.0, -168.0, 32.0, -3.0)
TIME_STEP = 0.45
REACH = len(COEFFS)
HALF = 64
F32, BF16 = jnp.float32, jnp.bfloat16
HIGHEST = lax.Precision.HIGHEST
VMEM = pl.BlockSpec(memory_space=pltpu.VMEM)
SMEM = pl.BlockSpec(memory_space=pltpu.SMEM)
ANY = pl.BlockSpec(memory_space=pl.ANY)
HBM = pl.BlockSpec(memory_space=pltpu.HBM)


def call(kernel, out_shapes, in_specs, args, scratch=(), room=16, out_spec=VMEM):
    return pl.pallas_call(
        kernel,
        out_shape=tuple(jax.ShapeDtypeStruct(s, d) for s, d in out_shapes),
        in_specs=in_specs,
        out_specs=tuple(out_spec for _ in out_shapes),
        scratch_shapes=list(scratch),
        compiler_params=pltpu.CompilerParams(vmem_limit_bytes=room * 2**20),
    )(*args)


def dot(a, b):
    return jnp.dot(a, b, preferred_element_type=F32)


def exact(a, b, dims=((1,), (0,))):
    return lax.dot_general(a, b, (dims, ((), ())), precision=HIGHEST, preferred_element_type=F32)


def split(x):
    high = x.astype(BF16)
    return high, (x - high.astype(F32)).astype(BF16)


def odd(axis):
    return lax.rem(lax.axis_index(axis), jnp.int32(2))


def rim_kernel(turn, f_ref, out_ref, sem):
    top, parity = f_ref.shape[1] - REACH, odd("gx")
    start = top * (parity if turn else 1 - parity)
    copy = pltpu.make_async_copy(f_ref.at[:, pl.ds(start, REACH)], out_ref, sem)
    copy.start()
    copy.wait()


def pack_rim(v, values, rim_ref):
    width = values.shape[2]
    group = lax.shift_right_logical(lax.broadcasted_iota(jnp.int32, values.shape, 2), 2)
    last = pltpu.roll(values, REACH * v + REACH, 2)
    first = pltpu.roll(values, width // 2 + REACH * v, 2)
    rim = jnp.where(group == v, last, rim_ref[...])
    rim_ref[...] = jnp.where(group == v + width // 2 // REACH, first, rim)


def pack_kernel(f_ref, rim_ref, same_ref, sems):
    count = f_ref.shape[0] // sems.shape[0]
    copies = []
    for i in range(sems.shape[0]):
        part = pl.ds(i * count, count)
        copies.append(pltpu.make_async_copy(f_ref.at[part], same_ref.at[part], sems.at[i]))
        copies[-1].start()
    rim_ref[...] = jnp.zeros_like(rim_ref)
    for i, copy in enumerate(copies):
        copy.wait()
        for v in range(i * count, (i + 1) * count):
            pack_rim(v, same_ref[v], rim_ref)


def iota(shape, dim):
    return lax.broadcasted_iota(jnp.int32, shape, dim)


def low_bits(x, size):
    return lax.rem(x, jnp.int32(size))


def weight_kernel(kin_ref, speed_ref, w_ref, dz_ref, shift_ref, scale_ref):
    nvars = kin_ref.shape[0]
    rows, columns = w_ref.shape[0] // 2, w_ref.shape[1]
    ny = rows // nvars
    spread = (iota((rows, nvars), 0) // ny == iota((rows, nvars), 1)).astype(F32)
    gather = (iota((nvars, columns), 1) // (2 * ny) == iota((nvars, columns), 0)).astype(F32)
    rates = exact(exact(spread, kin_ref[...]), gather)
    speed = exact(spread, speed_ref[...], ((1,), (1,)))[:, 1:2]
    row, column = iota((rows, columns), 0), iota((rows, columns), 1)
    y, other = low_bits(row, ny), low_bits(column, 2 * ny)
    iy = lax.axis_index("gy")
    below, above = iy > 0, iy < lax.axis_size("gy") - 1
    far = 8 * ny
    up = jnp.where(above, other - y, far)
    down = jnp.where(below, other - 2 * ny - y, far)
    offset = jnp.where(other < ny, other - y, jnp.where(other < ny + REACH, up, down))
    shifts = jnp.zeros((rows, columns), F32)
    for k in range(1, REACH + 1):
        shifts = jnp.where(offset == k, COEFFS[k - 1], jnp.where(offset == -k, -COEFFS[k - 1], shifts))
    shifts = jnp.where(row // ny == column // (2 * ny), speed * shifts, 0.0)
    high, low = split(TIME_STEP * (jnp.where(other == y, rates, 0.0) - shifts))
    w_ref[0:rows] = high
    w_ref[rows:] = low

    depth = dz_ref.shape[1]
    source, target = iota((depth, depth), 0), iota((depth, depth), 1)
    offset = source - target
    inner = jnp.zeros((depth, depth), F32)
    for k in range(1, REACH + 1):
        inner = jnp.where(offset == k, WHOLE[k - 1], jnp.where(offset == -k, -WHOLE[k - 1], inner))
    dz_ref[0:depth] = inner.astype(BF16)
    dz_ref[depth:] = inner.astype(BF16)
    turn = low_bits(target, REACH) - low_bits(source, REACH)
    first = source < depth // 2
    offset = REACH + jnp.where(first, turn, -turn)
    outer = jnp.zeros((depth, depth), F32)
    for k in range(1, REACH + 1):
        outer = jnp.where(offset == k, WHOLE[k - 1], outer)
    outer = jnp.where(source // REACH == target // REACH, jnp.where(first, -outer, outer), 0.0)
    shift_ref[...] = outer.astype(BF16)

    tile = scale_ref.shape[2:]
    for v in range(nvars):
        scale_ref[v, 0] = jnp.broadcast_to(TIME_STEP * speed_ref[0:1, v : v + 1], tile)
        scale_ref[v, 1] = jnp.broadcast_to(TIME_STEP / SCALE * speed_ref[2:3, v : v + 1], tile)


def project_kernel(zf_ref, zf_out_ref, wide_ref):
    depth, rank = zf_ref.shape[1], zf_ref.shape[0]
    identity = (iota((depth, depth), 0) == iota((depth, depth), 1)).astype(F32)
    wide_ref[...] = jnp.zeros_like(wide_ref)
    wide_ref[:, 0:rank] = exact(identity, zf_ref[...], ((1,), (1,)))
    high, low = split(wide_ref[...])
    zf_out_ref[0:depth, 0 : 2 * HALF] = high
    zf_out_ref[0:depth, 2 * HALF :] = low
    high, low = split(pltpu.roll(wide_ref[...], HALF, 1))
    zf_out_ref[depth:, 0 : 2 * HALF] = high
    zf_out_ref[depth:, 2 * HALF :] = low


def mix_planes(q_ref, beside_ref, w_ref, rate_ref):
    nvars, nx, ny, nz = q_ref.shape
    rows = nvars * ny

    def step(i, carry):
        high, low = [], []
        for p in (2 * i, 2 * i + 1):
            cells = jnp.concatenate([q_ref[:, p], beside_ref[:, p]], axis=1)
            h, l = split(cells.reshape(2 * rows, nz))
            high.append(h)
            low.append(l)
        both = dot(w_ref[...], jnp.concatenate(high, axis=1))
        total = both[:rows] + both[rows:] + dot(w_ref[0:rows], jnp.concatenate(low, axis=1))
        for j in range(2):
            rate_ref[:, 2 * i + j] = total[:, j * nz : (j + 1) * nz].reshape(nvars, ny, nz)
        return carry

    lax.fori_loop(0, nx // 2, step, 0, unroll=True)


def join_rims(first_ref, second_ref, shift_ref, rim_ref):
    nx, ny, nz = rim_ref.shape
    upper = lax.shift_right_logical(iota(rim_ref.shape, 2) * 2 // nz, 0)
    rim = jnp.where(upper == odd("gz"), second_ref[...], first_ref[...]).reshape(nx * ny, nz)
    high, low = split(rim)
    rim_ref[...] = (dot(high, shift_ref[...]) + dot(low, shift_ref[...])).reshape(rim_ref.shape)


def step_of(v, q_ref, first_ref, second_ref, dz_ref, rate_ref, rim_ref, scale_ref):
    _, nx, ny, nz = q_ref.shape
    q = q_ref[v]
    even = jnp.full((REACH, ny, nz), odd("gx")) == 0
    low_rim = jnp.where(even, second_ref[v], first_ref[v])
    high_rim = jnp.where(even, first_ref[v], second_ref[v])
    tall = jnp.concatenate([low_rim, q, high_rim], axis=0)
    gx = None
    for k in range(1, REACH + 1):
        part = COEFFS[k - 1] * (tall[REACH + k : REACH + k + nx] - tall[REACH - k : REACH - k + nx])
        gx = part if gx is None else gx + part
    high, low = split(q.reshape(nx * ny, nz))
    gz = dot(jnp.concatenate([high, low], axis=1), dz_ref[...]).reshape(nx, ny, nz)
    lane = lax.broadcasted_iota(jnp.int32, q.shape, 2)
    rim = rim_ref[...]
    first = pltpu.roll(rim, lax.rem(nz - REACH * v, nz), 2)
    last = pltpu.roll(rim, nz // 2 - REACH - REACH * v, 2)
    gz = gz + jnp.where(lane < REACH, first, jnp.where(lane >= nz - REACH, last, 0.0))
    return rate_ref[v] - scale_ref[v, 0] * gx - scale_ref[v, 1] * gz


def section_kernel(
    f_ref, x1_ref, x2_ref, beside_ref, z1_ref, z2_ref, w_ref, dz_ref, shift_ref, scale_ref,
    s_ref, first_ref, second_ref, out_rim_ref, rate_ref, rim_ref,
):
    mix_planes(f_ref, beside_ref, w_ref, rate_ref)
    join_rims(z1_ref, z2_ref, shift_ref, rim_ref)
    out_rim_ref[...] = jnp.zeros_like(out_rim_ref)

    def step(v, carry):
        s = f_ref[v] + step_of(v, f_ref, x1_ref, x2_ref, dz_ref, rate_ref, rim_ref, scale_ref)
        s_ref[v] = s
        low, high = s[:REACH], s[s.shape[0] - REACH :]
        even = jnp.full(low.shape, odd("gx")) == 0
        first_ref[v] = jnp.where(even, high, low)
        second_ref[v] = jnp.where(even, low, high)
        pack_rim(v, s, out_rim_ref)
        return carry

    lax.fori_loop(0, f_ref.shape[0], step, 0, unroll=4)


def next_kernel(
    f_ref, s_ref, x1_ref, x2_ref, beside_ref, z1_ref, z2_ref, w_ref, dz_ref, shift_ref, scale_ref, zf_ref,
    next_ref, *refs,
):
    _, nx, ny, nz = f_ref.shape
    chunk_refs, (rate_ref, rim_ref) = refs[:-2], refs[-2:]
    mix_planes(s_ref, beside_ref, w_ref, rate_ref)
    join_rims(z1_ref, z2_ref, shift_ref, rim_ref)
    count, pairs = len(chunk_refs), chunk_refs[0].shape[0]
    for k, chunk_ref in enumerate(chunk_refs):
        start = lax.rem(lax.axis_index("gz") + k, jnp.int32(count)) * (2 * pairs)
        for j in range(pairs):
            both = []
            for v in (start + 2 * j, start + 2 * j + 1):
                rate = step_of(v, s_ref, x1_ref, x2_ref, dz_ref, rate_ref, rim_ref, scale_ref)
                new = 0.5 * (f_ref[v] + s_ref[v] + rate)
                next_ref[v] = new
                both.append(new.reshape(nx * ny, nz))
            high, low = split(jnp.concatenate(both, axis=1))
            wide = dot(high, zf_ref[...])
            chunk_ref[j] = wide[:, : 2 * HALF] + wide[:, 2 * HALF :] + dot(low, zf_ref[:, : 2 * HALF])


def sum_kernel(*refs):
    total = refs[0][...]
    for ref in refs[1:-1]:
        total = total + ref[...]
    refs[-1][...] = total


def store_kernel(in_ref, out_ref, sem):
    copy = pltpu.make_async_copy(in_ref, out_ref, sem)
    copy.start()
    copy.wait()


def factor_kernel(rank_ref, xf_ref, *refs):
    y_refs, out_ref = refs[:-1], refs[-1]
    blocks, _, rows, width = out_ref.shape
    ny = y_refs[0].shape[0]
    nx = rank_ref.shape[1] // blocks
    a_count = xf_ref.shape[1] // lax.axis_size("gx")
    b_count = rows // a_count

    def own(count, total, place):
        return (iota((count, total), 1) == iota((count, total), 0) + place * count).astype(F32)

    mine = exact(own(a_count, xf_ref.shape[1], lax.axis_index("gx")), xf_ref[...], ((1,), (1,)))
    pick = iota((xf_ref.shape[0], rank_ref.shape[1]), 0) == rank_ref[...]
    mine = exact(mine, pick.astype(F32))
    column = iota((nx, width), 1)
    spread_x = (iota((nx, width), 0) == low_bits(column // ny, nx)).astype(F32)
    column = iota((ny, width), 1)
    yt = None
    for j, y_ref in enumerate(y_refs):
        mine_y = exact(own(b_count, y_ref.shape[1], lax.axis_index("gy")), y_ref[...], ((1,), (1,)))
        here = (iota((ny, width), 0) == low_bits(column, ny)) & (column // (nx * ny) == j)
        part = exact(mine_y, here.astype(F32))
        yt = part if yt is None else yt + part
    for i in range(blocks):
        xt = exact(mine[:, i * nx : (i + 1) * nx], spread_x)
        for a in range(a_count):
            high, low = split(xt[a : a + 1, :] * yt)
            out_ref[i, 0, a * b_count : (a + 1) * b_count] = high
            out_ref[i, 1, a * b_count : (a + 1) * b_count] = low


def contracted(factor_ref, i, block_refs):
    pairs = block_refs[0].shape[0]
    columns = [jnp.concatenate([r[p] for r in block_refs], axis=0) for p in range(pairs)]
    high, low = split(jnp.concatenate(columns, axis=1))
    q_high, q_low = factor_ref[i, 0], factor_ref[i, 1]
    return dot(q_high, high) + (dot(q_high, low) + dot(q_low, high))


def early_kernel(blocks_y, factor_ref, *refs):
    total = None
    for i in range((len(refs) - 1) // blocks_y):
        part = contracted(factor_ref, i, refs[i * blocks_y : (i + 1) * blocks_y])
        total = part if total is None else total + part
    refs[-1][...] = total


def core_kernel(factor_ref, total_ref, *refs):
    out_ref = refs[-1]
    rank = out_ref.shape[2]
    result = total_ref[...] + contracted(factor_ref, factor_ref.shape[0] - 1, refs[:-1])
    for v in range(out_ref.shape[0]):
        out_ref[v] = result[:, v * HALF : v * HALF + rank]


def shifted(x, axis, k):
    count = lax.axis_size(axis)
    return lax.ppermute(x, axis, [(i, (i + k) % count) for i in range(count)])


def gathered(x, axis):
    count = lax.axis_size(axis)
    if count <= 4:
        return [x] + [shifted(x, axis, k) for k in range(1, count)]
    blocks = lax.all_gather(x, axis)
    return [blocks[k] for k in range(count)]


def gathered_on_chip(x):
    count = lax.axis_size("gx")
    if count != 4 or lax.axis_size("gy") != 2:
        return gathered(x, "gx")
    ring = [((i, j), ((i + (1, 3)[j]) % 4, j)) for i in range(4) for j in range(2)]
    mine = lax.ppermute(x, ("gx", "gy"), [(2 * i + j, 2 * k + l) for (i, j), (k, l) in ring])
    across = shifted(x, "gx", 2)
    theirs = lax.ppermute(mine, "gy", [(0, 1), (1, 0)])
    upper = lax.axis_index("gy") == 1
    return [x, jnp.where(upper, theirs, mine), across, jnp.where(upper, mine, theirs)]


def paired(first, second, axis):
    out = []
    for x, start in ((first, 0), (second, 1)):
        links = [(i, i + 1) for i in range(start, lax.axis_size(axis) - 1, 2)]
        out.append(lax.ppermute(x, axis, links + [(j, i) for i, j in links]))
    return out


def beside(block, axis):
    count = lax.axis_size(axis)
    if count == 2:
        return lax.ppermute(block, axis, [(0, 1), (1, 0)])
    from_low = lax.ppermute(block, axis, [(i, i + 1) for i in range(count - 1)])
    from_high = lax.ppermute(block, axis, [(i + 1, i) for i in range(count - 1)])
    row = lax.broadcasted_iota(jnp.int32, block.shape, 2)
    return jnp.where(row < REACH, from_high, from_low)


def local(fields, speeds, kinetics, block_rank, x_factor, y_factor, z_factor):
    nvars, nx, ny, nz = fields.shape
    rank = z_factor.shape[1]
    gx, gy, gz = (lax.axis_size(axis) for axis in ("gx", "gy", "gz"))
    rim = (nvars, REACH, ny, nz)
    plane = (nx, ny, nz)
    scratch = [pltpu.VMEM(fields.shape, F32), pltpu.VMEM(plane, F32)]
    pairs = nvars // 2 // gz
    chunk = (pairs, nx * ny, 2 * HALF)
    barrier = lax.optimization_barrier

    first, second = (
        call(functools.partial(rim_kernel, turn), [(rim, F32)], [HBM], (fields,), [pltpu.SemaphoreType.DMA])[0]
        for turn in (0, 1)
    )
    x1, x2 = paired(first, second, "gx")
    packed, same = call(
        pack_kernel, [(plane, F32), (fields.shape, F32)], [HBM], (fields,), [pltpu.SemaphoreType.DMA((4,))]
    )
    z1, z2 = paired(packed, packed, "gz")
    other = beside(fields, "gy")
    weights, dz, rim_shift, scales = call(
        weight_kernel,
        [((2 * nvars * ny, 2 * nvars * ny), BF16), ((2 * nz, nz), BF16), ((nz, nz), BF16), ((nvars, 2, ny, nz), F32)],
        [VMEM] * 2,
        (kinetics, speeds),
    )
    section, first, second, packed = call(
        section_kernel,
        [(fields.shape, F32), (rim, F32), (rim, F32), (plane, F32)],
        [VMEM] * 10,
        (same, x1, x2, other, z1, z2, weights, dz, rim_shift, scales),
        scratch,
    )
    a_count, b_count = x_factor.shape[1] // gx, y_factor.shape[1] // gy
    rows, planes = a_count * b_count, gx * nx
    cells = planes * gy * ny
    section, first, second, packed, z_factor, x_factor, y_factor = barrier(
        (section, first, second, packed, z_factor, x_factor, y_factor)
    )
    x1, x2 = paired(first, second, "gx")
    z1, z2 = paired(packed, packed, "gz")
    other = beside(section, "gy")
    y_rows = gathered(y_factor, "gy")
    (zf,) = call(project_kernel, [((2 * nz, 4 * HALF), BF16)], [VMEM], (z_factor.T,), [pltpu.VMEM((nz, 2 * HALF), F32)])
    x1, x2, z1, z2, other, zf = barrier((x1, x2, z1, z2, other, zf))
    new, *chunks = call(
        next_kernel,
        [(fields.shape, F32)] + [(chunk, F32)] * gz,
        [VMEM] * 12,
        (same, section, x1, x2, other, z1, z2, weights, dz, rim_shift, scales, zf),
        scratch,
    )
    new, chunks, block_rank = barrier((new, chunks, block_rank))
    parts = [chunks[0]] + [shifted(chunks[k], "gz", k) for k in range(1, gz)]
    ranks = jnp.concatenate(gathered_on_chip(block_rank.reshape(1, nx)), axis=1)
    (fields_next,) = call(store_kernel, [(fields.shape, F32)], [ANY], (new,), [pltpu.SemaphoreType.DMA], out_spec=HBM)
    (factor,) = call(
        factor_kernel,
        [((gx, 2, rows, gy * nx * ny), BF16)],
        [VMEM] * (2 + gy),
        (ranks, x_factor, *y_rows),
        room=16 if cells <= 1024 else 56,
    )
    (own,) = call(sum_kernel, [(chunk, F32)], [VMEM] * gz, parts)
    *blocks, last = gathered(own, "gx")
    blocks = [gathered(block, "gy") for block in blocks]
    blocks.append(gathered(last, "gy"))
    room = 16 if cells <= 1024 else 56
    early = [block for line in blocks[:-1] for block in line]
    (total,) = call(
        functools.partial(early_kernel, gy),
        [((rows, 2 * pairs * HALF), F32)],
        [VMEM] * (1 + len(early)),
        (factor, *early),
        room=room,
    )
    (core,) = call(
        core_kernel,
        [((2 * pairs, rows, rank), F32)],
        [VMEM] * (2 + gy),
        (factor, total, *blocks[-1]),
        room=room,
    )
    return fields_next, core.reshape(2 * pairs, a_count, b_count, rank)


def solution(mesh):
    placed = (P(None, "gx", "gy", "gz"), P(), P(), P("gx"), P(), P("gy", None), P("gz", None))
    return jax.shard_map(
        local,
        mesh=mesh,
        in_specs=placed,
        out_specs=(P(None, "gx", "gy", "gz"), P("gz", "gx", "gy", None)),
        check_vma=False,
    )
```

```python
import functools

import jax
import jax.numpy as jnp
from jax import lax
from jax.experimental import pallas as pl
from jax.experimental.pallas import tpu as pltpu
from jax.sharding import PartitionSpec as P

COEFFS = (0.8, -0.2, 4.0 / 105.0, -1.0 / 280.0)
SCALE = 840.0
WHOLE = (672.0, -168.0, 32.0, -3.0)
TIME_STEP = 0.45
REACH = len(COEFFS)
HALF = 64
F32, BF16 = jnp.float32, jnp.bfloat16
HIGHEST = lax.Precision.HIGHEST
VMEM = pl.BlockSpec(memory_space=pltpu.VMEM)
SMEM = pl.BlockSpec(memory_space=pltpu.SMEM)
ANY = pl.BlockSpec(memory_space=pl.ANY)
HBM = pl.BlockSpec(memory_space=pltpu.HBM)


def call(kernel, out_shapes, in_specs, args, scratch=(), room=16, out_spec=VMEM):
    return pl.pallas_call(
        kernel,
        out_shape=tuple(jax.ShapeDtypeStruct(s, d) for s, d in out_shapes),
        in_specs=in_specs,
        out_specs=tuple(out_spec for _ in out_shapes),
        scratch_shapes=list(scratch),
        compiler_params=pltpu.CompilerParams(vmem_limit_bytes=room * 2**20),
    )(*args)


def dot(a, b):
    return jnp.dot(a, b, preferred_element_type=F32)


def exact(a, b, dims=((1,), (0,))):
    return lax.dot_general(a, b, (dims, ((), ())), precision=HIGHEST, preferred_element_type=F32)


def split(x):
    high = x.astype(BF16)
    return high, (x - high.astype(F32)).astype(BF16)


def odd(axis):
    return lax.rem(lax.axis_index(axis), jnp.int32(2))


def rim_kernel(f_ref, first_ref, second_ref, sems):
    top, parity = f_ref.shape[1] - REACH, odd("gx")
    copies = [
        pltpu.make_async_copy(f_ref.at[:, pl.ds(start, REACH)], target, sems.at[i])
        for i, (start, target) in enumerate(((top * (1 - parity), first_ref), (top * parity, second_ref)))
    ]
    for copy in copies:
        copy.start()
    for copy in copies:
        copy.wait()


def pack_rim(v, values, rim_ref):
    width = values.shape[2]
    group = lax.shift_right_logical(lax.broadcasted_iota(jnp.int32, values.shape, 2), 2)
    last = pltpu.roll(values, REACH * v + REACH, 2)
    first = pltpu.roll(values, width // 2 + REACH * v, 2)
    rim = jnp.where(group == v, last, rim_ref[...])
    rim_ref[...] = jnp.where(group == v + width // 2 // REACH, first, rim)


def pack_kernel(f_ref, rim_ref, same_ref, sems):
    count = f_ref.shape[0] // sems.shape[0]
    copies = []
    for i in range(sems.shape[0]):
        part = pl.ds(i * count, count)
        copies.append(pltpu.make_async_copy(f_ref.at[part], same_ref.at[part], sems.at[i]))
        copies[-1].start()
    rim_ref[...] = jnp.zeros_like(rim_ref)
    for i, copy in enumerate(copies):
        copy.wait()
        for v in range(i * count, (i + 1) * count):
            pack_rim(v, same_ref[v], rim_ref)


def iota(shape, dim):
    return lax.broadcasted_iota(jnp.int32, shape, dim)


def low_bits(x, size):
    return lax.rem(x, jnp.int32(size))


def weight_kernel(kin_ref, speed_ref, w_ref, dz_ref, shift_ref, scale_ref):
    nvars = kin_ref.shape[0]
    rows, columns = w_ref.shape[0] // 2, w_ref.shape[1]
    ny = rows // nvars
    spread = (iota((rows, nvars), 0) // ny == iota((rows, nvars), 1)).astype(F32)
    gather = (iota((nvars, columns), 1) // (2 * ny) == iota((nvars, columns), 0)).astype(F32)
    rates = exact(exact(spread, kin_ref[...]), gather)
    speed = exact(spread, speed_ref[...], ((1,), (1,)))[:, 1:2]
    row, column = iota((rows, columns), 0), iota((rows, columns), 1)
    y, other = low_bits(row, ny), low_bits(column, 2 * ny)
    iy = lax.axis_index("gy")
    below, above = iy > 0, iy < lax.axis_size("gy") - 1
    far = 8 * ny
    up = jnp.where(above, other - y, far)
    down = jnp.where(below, other - 2 * ny - y, far)
    offset = jnp.where(other < ny, other - y, jnp.where(other < ny + REACH, up, down))
    shifts = jnp.zeros((rows, columns), F32)
    for k in range(1, REACH + 1):
        shifts = jnp.where(offset == k, COEFFS[k - 1], jnp.where(offset == -k, -COEFFS[k - 1], shifts))
    shifts = jnp.where(row // ny == column // (2 * ny), speed * shifts, 0.0)
    high, low = split(TIME_STEP * (jnp.where(other == y, rates, 0.0) - shifts))
    w_ref[0:rows] = high
    w_ref[rows:] = low

    depth = dz_ref.shape[1]
    source, target = iota((depth, depth), 0), iota((depth, depth), 1)
    offset = source - target
    inner = jnp.zeros((depth, depth), F32)
    for k in range(1, REACH + 1):
        inner = jnp.where(offset == k, WHOLE[k - 1], jnp.where(offset == -k, -WHOLE[k - 1], inner))
    dz_ref[0:depth] = inner.astype(BF16)
    dz_ref[depth:] = inner.astype(BF16)
    turn = low_bits(target, REACH) - low_bits(source, REACH)
    first = source < depth // 2
    offset = REACH + jnp.where(first, turn, -turn)
    outer = jnp.zeros((depth, depth), F32)
    for k in range(1, REACH + 1):
        outer = jnp.where(offset == k, WHOLE[k - 1], outer)
    outer = jnp.where(source // REACH == target // REACH, jnp.where(first, -outer, outer), 0.0)
    shift_ref[...] = outer.astype(BF16)

    tile = scale_ref.shape[2:]
    for v in range(nvars):
        scale_ref[v, 0] = jnp.broadcast_to(TIME_STEP * speed_ref[0:1, v : v + 1], tile)
        scale_ref[v, 1] = jnp.broadcast_to(TIME_STEP / SCALE * speed_ref[2:3, v : v + 1], tile)


def project_kernel(zf_ref, zf_out_ref, wide_ref):
    depth, rank = zf_ref.shape[1], zf_ref.shape[0]
    identity = (iota((depth, depth), 0) == iota((depth, depth), 1)).astype(F32)
    wide_ref[...] = jnp.zeros_like(wide_ref)
    wide_ref[:, 0:rank] = exact(identity, zf_ref[...], ((1,), (1,)))
    high, low = split(wide_ref[...])
    zf_out_ref[0:depth, 0 : 2 * HALF] = high
    zf_out_ref[0:depth, 2 * HALF :] = low
    high, low = split(pltpu.roll(wide_ref[...], HALF, 1))
    zf_out_ref[depth:, 0 : 2 * HALF] = high
    zf_out_ref[depth:, 2 * HALF :] = low


def mix_planes(q_ref, beside_ref, w_ref, rate_ref):
    nvars, nx, ny, nz = q_ref.shape
    rows = nvars * ny

    def step(i, carry):
        high, low = [], []
        for p in (2 * i, 2 * i + 1):
            cells = jnp.concatenate([q_ref[:, p], beside_ref[:, p]], axis=1)
            h, l = split(cells.reshape(2 * rows, nz))
            high.append(h)
            low.append(l)
        both = dot(w_ref[...], jnp.concatenate(high, axis=1))
        total = both[:rows] + both[rows:] + dot(w_ref[0:rows], jnp.concatenate(low, axis=1))
        for j in range(2):
            rate_ref[:, 2 * i + j] = total[:, j * nz : (j + 1) * nz].reshape(nvars, ny, nz)
        return carry

    lax.fori_loop(0, nx // 2, step, 0, unroll=True)


def join_rims(first_ref, second_ref, shift_ref, rim_ref):
    nx, ny, nz = rim_ref.shape
    upper = lax.shift_right_logical(iota(rim_ref.shape, 2) * 2 // nz, 0)
    rim = jnp.where(upper == odd("gz"), second_ref[...], first_ref[...]).reshape(nx * ny, nz)
    high, low = split(rim)
    rim_ref[...] = (dot(high, shift_ref[...]) + dot(low, shift_ref[...])).reshape(rim_ref.shape)


def step_of(v, q_ref, first_ref, second_ref, dz_ref, rate_ref, rim_ref, scale_ref):
    _, nx, ny, nz = q_ref.shape
    q = q_ref[v]
    even = jnp.full((REACH, ny, nz), odd("gx")) == 0
    low_rim = jnp.where(even, second_ref[v], first_ref[v])
    high_rim = jnp.where(even, first_ref[v], second_ref[v])
    tall = jnp.concatenate([low_rim, q, high_rim], axis=0)
    gx = None
    for k in range(1, REACH + 1):
        part = COEFFS[k - 1] * (tall[REACH + k : REACH + k + nx] - tall[REACH - k : REACH - k + nx])
        gx = part if gx is None else gx + part
    high, low = split(q.reshape(nx * ny, nz))
    gz = dot(jnp.concatenate([high, low], axis=1), dz_ref[...]).reshape(nx, ny, nz)
    lane = lax.broadcasted_iota(jnp.int32, q.shape, 2)
    rim = rim_ref[...]
    first = pltpu.roll(rim, lax.rem(nz - REACH * v, nz), 2)
    last = pltpu.roll(rim, nz // 2 - REACH - REACH * v, 2)
    gz = gz + jnp.where(lane < REACH, first, jnp.where(lane >= nz - REACH, last, 0.0))
    return rate_ref[v] - scale_ref[v, 0] * gx - scale_ref[v, 1] * gz


def section_kernel(
    f_ref, x1_ref, x2_ref, beside_ref, z1_ref, z2_ref, w_ref, dz_ref, shift_ref, scale_ref,
    s_ref, first_ref, second_ref, out_rim_ref, rate_ref, rim_ref,
):
    mix_planes(f_ref, beside_ref, w_ref, rate_ref)
    join_rims(z1_ref, z2_ref, shift_ref, rim_ref)
    out_rim_ref[...] = jnp.zeros_like(out_rim_ref)

    def step(v, carry):
        s = f_ref[v] + step_of(v, f_ref, x1_ref, x2_ref, dz_ref, rate_ref, rim_ref, scale_ref)
        s_ref[v] = s
        low, high = s[:REACH], s[s.shape[0] - REACH :]
        even = jnp.full(low.shape, odd("gx")) == 0
        first_ref[v] = jnp.where(even, high, low)
        second_ref[v] = jnp.where(even, low, high)
        pack_rim(v, s, out_rim_ref)
        return carry

    lax.fori_loop(0, f_ref.shape[0], step, 0, unroll=4)


def next_kernel(
    f_ref, s_ref, x1_ref, x2_ref, beside_ref, z1_ref, z2_ref, w_ref, dz_ref, shift_ref, scale_ref, zf_ref,
    next_ref, *refs,
):
    _, nx, ny, nz = f_ref.shape
    chunk_refs, (rate_ref, rim_ref) = refs[:-2], refs[-2:]
    mix_planes(s_ref, beside_ref, w_ref, rate_ref)
    join_rims(z1_ref, z2_ref, shift_ref, rim_ref)
    count, pairs = len(chunk_refs), chunk_refs[0].shape[0]
    for k, chunk_ref in enumerate(chunk_refs):
        start = lax.rem(lax.axis_index("gz") + k, jnp.int32(count)) * (2 * pairs)
        for j in range(pairs):
            both = []
            for v in (start + 2 * j, start + 2 * j + 1):
                rate = step_of(v, s_ref, x1_ref, x2_ref, dz_ref, rate_ref, rim_ref, scale_ref)
                new = 0.5 * (f_ref[v] + s_ref[v] + rate)
                next_ref[v] = new
                both.append(new.reshape(nx * ny, nz))
            high, low = split(jnp.concatenate(both, axis=1))
            wide = dot(high, zf_ref[...])
            chunk_ref[j] = wide[:, : 2 * HALF] + wide[:, 2 * HALF :] + dot(low, zf_ref[:, : 2 * HALF])


def sum_kernel(*refs):
    total = refs[0][...]
    for ref in refs[1:-1]:
        total = total + ref[...]
    refs[-1][...] = total


def store_kernel(in_ref, out_ref, sem):
    copy = pltpu.make_async_copy(in_ref, out_ref, sem)
    copy.start()
    copy.wait()


def factor_kernel(rank_ref, xf_ref, *refs):
    y_refs, out_ref = refs[:-1], refs[-1]
    blocks, _, rows, width = out_ref.shape
    ny = y_refs[0].shape[0]
    nx = rank_ref.shape[1] // blocks
    a_count = xf_ref.shape[1] // lax.axis_size("gx")
    b_count = rows // a_count

    def own(count, total, place):
        return (iota((count, total), 1) == iota((count, total), 0) + place * count).astype(F32)

    mine = exact(own(a_count, xf_ref.shape[1], lax.axis_index("gx")), xf_ref[...], ((1,), (1,)))
    pick = iota((xf_ref.shape[0], rank_ref.shape[1]), 0) == rank_ref[...]
    mine = exact(mine, pick.astype(F32))
    column = iota((nx, width), 1)
    spread_x = (iota((nx, width), 0) == low_bits(column // ny, nx)).astype(F32)
    column = iota((ny, width), 1)
    yt = None
    for j, y_ref in enumerate(y_refs):
        mine_y = exact(own(b_count, y_ref.shape[1], lax.axis_index("gy")), y_ref[...], ((1,), (1,)))
        here = (iota((ny, width), 0) == low_bits(column, ny)) & (column // (nx * ny) == j)
        part = exact(mine_y, here.astype(F32))
        yt = part if yt is None else yt + part
    for i in range(blocks):
        xt = exact(mine[:, i * nx : (i + 1) * nx], spread_x)
        for a in range(a_count):
            high, low = split(xt[a : a + 1, :] * yt)
            out_ref[i, 0, a * b_count : (a + 1) * b_count] = high
            out_ref[i, 1, a * b_count : (a + 1) * b_count] = low


def contracted(factor_ref, i, block_refs):
    pairs = block_refs[0].shape[0]
    columns = [jnp.concatenate([r[p] for r in block_refs], axis=0) for p in range(pairs)]
    high, low = split(jnp.concatenate(columns, axis=1))
    q_high, q_low = factor_ref[i, 0], factor_ref[i, 1]
    return dot(q_high, high) + (dot(q_high, low) + dot(q_low, high))


def early_kernel(blocks_y, factor_ref, *refs):
    total = None
    for i in range((len(refs) - 1) // blocks_y):
        part = contracted(factor_ref, i, refs[i * blocks_y : (i + 1) * blocks_y])
        total = part if total is None else total + part
    refs[-1][...] = total


def core_kernel(factor_ref, total_ref, *refs):
    out_ref = refs[-1]
    rank = out_ref.shape[2]
    result = total_ref[...] + contracted(factor_ref, factor_ref.shape[0] - 1, refs[:-1])
    for v in range(out_ref.shape[0]):
        out_ref[v] = result[:, v * HALF : v * HALF + rank]


def shifted(x, axis, k):
    count = lax.axis_size(axis)
    return lax.ppermute(x, axis, [(i, (i + k) % count) for i in range(count)])


def swapped(x, axis, k):
    return lax.ppermute(x, axis, [(i, i ^ k) for i in range(lax.axis_size(axis))])


def gathered(x, axis):
    count = lax.axis_size(axis)
    if count in (2, 4):
        return [x] + [swapped(x, axis, k) for k in range(1, count)]
    blocks = lax.all_gather(x, axis)
    return [blocks[k] for k in range(count)]


def gathered_on_chip(x):
    count = lax.axis_size("gx")
    if count != 4 or lax.axis_size("gy") != 2:
        return gathered(x, "gx")
    links = [(2 * i + j, 2 * (i ^ (j + 1)) + j) for i in range(4) for j in range(2)]
    mine = lax.ppermute(x, ("gx", "gy"), links)
    across = swapped(x, "gx", 3)
    theirs = lax.ppermute(mine, "gy", [(0, 1), (1, 0)])
    upper = lax.axis_index("gy") == 1
    return [x, jnp.where(upper, theirs, mine), jnp.where(upper, mine, theirs), across]


def paired(first, second, axis):
    out = []
    for x, start in ((first, 0), (second, 1)):
        links = [(i, i + 1) for i in range(start, lax.axis_size(axis) - 1, 2)]
        out.append(lax.ppermute(x, axis, links + [(j, i) for i, j in links]))
    return out


def beside(block, axis):
    count = lax.axis_size(axis)
    if count == 2:
        return lax.ppermute(block, axis, [(0, 1), (1, 0)])
    from_low = lax.ppermute(block, axis, [(i, i + 1) for i in range(count - 1)])
    from_high = lax.ppermute(block, axis, [(i + 1, i) for i in range(count - 1)])
    row = lax.broadcasted_iota(jnp.int32, block.shape, 2)
    return jnp.where(row < REACH, from_high, from_low)


def local(fields, speeds, kinetics, block_rank, x_factor, y_factor, z_factor):
    nvars, nx, ny, nz = fields.shape
    rank = z_factor.shape[1]
    gx, gy, gz = (lax.axis_size(axis) for axis in ("gx", "gy", "gz"))
    rim = (nvars, REACH, ny, nz)
    plane = (nx, ny, nz)
    scratch = [pltpu.VMEM(fields.shape, F32), pltpu.VMEM(plane, F32)]
    pairs = nvars // 2 // gz
    chunk = (pairs, nx * ny, 2 * HALF)
    barrier = lax.optimization_barrier

    first, second = call(
        rim_kernel, [(rim, F32), (rim, F32)], [HBM], (fields,), [pltpu.SemaphoreType.DMA((2,))]
    )
    x1, x2 = paired(first, second, "gx")
    packed, same = call(
        pack_kernel, [(plane, F32), (fields.shape, F32)], [HBM], (fields,), [pltpu.SemaphoreType.DMA((4,))]
    )
    z1, z2 = paired(packed, packed, "gz")
    other = beside(fields, "gy")
    weights, dz, rim_shift, scales = call(
        weight_kernel,
        [((2 * nvars * ny, 2 * nvars * ny), BF16), ((2 * nz, nz), BF16), ((nz, nz), BF16), ((nvars, 2, ny, nz), F32)],
        [VMEM] * 2,
        (kinetics, speeds),
    )
    section, first, second, packed = call(
        section_kernel,
        [(fields.shape, F32), (rim, F32), (rim, F32), (plane, F32)],
        [VMEM] * 10,
        (same, x1, x2, other, z1, z2, weights, dz, rim_shift, scales),
        scratch,
    )
    a_count, b_count = x_factor.shape[1] // gx, y_factor.shape[1] // gy
    rows, planes = a_count * b_count, gx * nx
    cells = planes * gy * ny
    section, first, second, packed, z_factor, x_factor, y_factor = barrier(
        (section, first, second, packed, z_factor, x_factor, y_factor)
    )
    x1, x2 = paired(first, second, "gx")
    z1, z2 = paired(packed, packed, "gz")
    other = beside(section, "gy")
    y_rows = gathered(y_factor, "gy")
    (zf,) = call(project_kernel, [((2 * nz, 4 * HALF), BF16)], [VMEM], (z_factor.T,), [pltpu.VMEM((nz, 2 * HALF), F32)])
    x1, x2, z1, z2, other, zf = barrier((x1, x2, z1, z2, other, zf))
    new, *chunks = call(
        next_kernel,
        [(fields.shape, F32)] + [(chunk, F32)] * gz,
        [VMEM] * 12,
        (same, section, x1, x2, other, z1, z2, weights, dz, rim_shift, scales, zf),
        scratch,
    )
    new, chunks, block_rank = barrier((new, chunks, block_rank))
    parts = [chunks[0]] + [shifted(chunks[k], "gz", k) for k in range(1, gz)]
    ranks = jnp.concatenate(gathered_on_chip(block_rank.reshape(1, nx)), axis=1)
    (fields_next,) = call(store_kernel, [(fields.shape, F32)], [ANY], (new,), [pltpu.SemaphoreType.DMA], out_spec=HBM)
    (factor,) = call(
        factor_kernel,
        [((gx, 2, rows, gy * nx * ny), BF16)],
        [VMEM] * (2 + gy),
        (ranks, x_factor, *y_rows),
        room=16 if cells <= 1024 else 56,
    )
    (own,) = call(sum_kernel, [(chunk, F32)], [VMEM] * gz, parts)
    *blocks, last = gathered(own, "gx")
    blocks = [gathered(block, "gy") for block in blocks]
    blocks.append(gathered(last, "gy"))
    room = 16 if cells <= 1024 else 56
    early = [block for line in blocks[:-1] for block in line]
    (total,) = call(
        functools.partial(early_kernel, gy),
        [((rows, 2 * pairs * HALF), F32)],
        [VMEM] * (1 + len(early)),
        (factor, *early),
        room=room,
    )
    (core,) = call(
        core_kernel,
        [((2 * pairs, rows, rank), F32)],
        [VMEM] * (2 + gy),
        (factor, total, *blocks[-1]),
        room=room,
    )
    return fields_next, core.reshape(2 * pairs, a_count, b_count, rank)


def solution(mesh):
    placed = (P(None, "gx", "gy", "gz"), P(), P(), P("gx"), P(), P("gy", None), P("gz", None))
    return jax.shard_map(
        local,
        mesh=mesh,
        in_specs=placed,
        out_specs=(P(None, "gx", "gy", "gz"), P("gz", "gx", "gy", None)),
        check_vma=False,
    )
```
